128 devices in a mesh: cells: 64 (over y, z, x), members: 2 (over core).
Axes of the slice: x: 4, y: 4, z: 4, core: 2. Of those that a mesh axis runs over, the one named last changes fastest.
Arguments:
- ensemble: float32 [64, 4, 65536], P('members', None, 'cells')
- speed: float32 [65536], P('cells'), may hold values from 0.1 to 0.85
- direction: int32 [65536], P('cells'), may hold values 0 or 1
- couple: float32 [4, 4], replicated, may hold values from -0.25 to 0.25
- obs_place: int32 [16384], P('cells'), may hold values from 0 to 1023
- obs_field: int32 [16384], P('cells'), may hold values from 0 to 3
- obs_value: float32 [16384], P('cells'), may hold values from -8 to 8
- obs_sigma: float32 [16384], P('cells'), may hold values from 0.5 to 5
- send_count: int32 [64, 64], P('cells'), may hold values from 0 to 32, as said below
Outputs:
- analysis: float32 [64, 4, 65536], P('members', None, 'cells')
- innovation: float32 [16384], P('cells')
The draws below stay inside these ranges and needn't reach their ends.
Inputs may be any that keep to these rules, and one draw needn't show every extreme that they name: Each row of send_count sums to 256; no entry exceeds 32; in every row four blocks get exactly 32, and one block gets exactly 32 from every row.
All inputs are finite; a program needn't handle non-finite values. No bound on the sum of `direction` on one device may be relied on, other than what follows from the above.
Results may differ from the reference program's by a relative error of at most 0.0001.
Values sent between devices are 32-bit elements; how exact they have to be, the bound alone decides.
A program may use at most 64 MiB of HBM per device.

```python
import math
import jax
import jax.numpy as jnp
from jax import lax

F = 4
K = 64
STEPS = 4
CELLS_DEV = 1024
OBS_DEV = 256
CAP = 32
OWNERS = 64
NC = 65536
NOBS = 16384


def draw_ensemble(key, part):
    key_noise, key_rough, key_center = jax.random.split(key, 3)
    position = jnp.arange(NC, dtype=jnp.float32) / NC
    rising = jnp.exp(jnp.log(3.0) * position)
    center = jax.random.normal(key_center, (1, F, NC), jnp.float32)
    roughness = jnp.exp(jax.random.uniform(key_rough, (1, F, NC), jnp.float32, -0.7, 0.7))
    noise_draw = jnp.clip(jax.random.normal(key_noise, (K, F, NC), jnp.float32), -4.0, 4.0)
    return center + rising * roughness * noise_draw


def draw_send_count(key, part):
    base_key = jax.random.fold_in(key, 11)
    key_hot, key_pick, key_spread = jax.random.split(base_key, 3)
    hottest = jax.random.permutation(key_hot, OWNERS)[:8]
    pick_keys = jax.random.split(key_pick, OWNERS)
    picked = jax.vmap(lambda single_key: jax.random.permutation(single_key, 7)[:3] + 1)(pick_keys)
    chosen = jnp.concatenate([jnp.broadcast_to(hottest[:1], (OWNERS, 1)), hottest[picked]], axis=1)
    owner_ids = jnp.arange(OWNERS, dtype=jnp.int32)
    is_hot = jnp.any(owner_ids[None, :, None] == chosen[:, None, :], axis=2).astype(jnp.int32)
    ordering = jnp.argsort(is_hot * OWNERS + owner_ids[None, :], axis=1)
    spare_rows = OBS_DEV - 4 * CAP
    other_owners = OWNERS - 4
    spread_keys = jax.random.split(key_spread, OWNERS)

    def spread_row(single_key):
        slot_owner = jax.random.permutation(single_key, other_owners * CAP)[:spare_rows] // CAP
        return jnp.sum((slot_owner[:, None] == jnp.arange(other_owners, dtype=jnp.int32)[None, :]).astype(jnp.int32), axis=0)
    loads = jax.vmap(spread_row)(spread_keys).astype(jnp.int32)
    in_order = jnp.concatenate([loads, jnp.full((OWNERS, 4), CAP, jnp.int32)], axis=1)
    row_ids = jnp.broadcast_to(owner_ids[:, None], (OWNERS, OWNERS))
    return jnp.zeros((OWNERS, OWNERS), jnp.int32).at[row_ids, ordering].set(in_order)


def with_ends(entries, key, smallest, high):
    extent = entries.shape
    spot = [jax.random.randint(jax.random.fold_in(key, axis), (), 0, extent[axis]) for axis in range(len(extent))]
    entries = entries.at[tuple(spot)].set(smallest)
    longest = extent.index(max(extent))
    spot[longest] = (spot[longest] + 1) % extent[longest]
    return entries.at[tuple(spot)].set(high)


def block_scale(rng, dims, cuts, low, top_value):
    def one(axis_at, blocks):
        steps = jax.random.uniform(jax.random.fold_in(jax.random.fold_in(rng, 6), axis_at), (blocks,), jnp.float32, low / len(cuts), top_value / len(cuts))
        return jnp.repeat(jnp.exp(steps), dims[axis_at] // blocks).reshape((-1,) + (1,) * (len(dims) - axis_at - 1))

    loudness = one(*cuts[0])
    for cut in cuts[1:]:
        loudness = loudness * one(*cut)
    return loudness


def noise(key, extent, deviation, limit, pieces=(), kind=jnp.bfloat16):
    array = deviation * jax.random.normal(key, extent, jnp.float32)
    if pieces:
        array = array * block_scale(key, extent, pieces, -0.22, 0.18)
    return jnp.clip(array, -limit, limit).astype(kind)


def setup_inputs(seed: int = 0) -> dict:
    streams_of = jax.random.split(jax.random.key(seed), 10)
    ensemble = draw_ensemble(jax.random.fold_in(streams_of[9], 71), 0)
    speed = jnp.clip(jnp.exp(math.log(0.85) - 2.1400662 * jax.random.uniform(streams_of[1], (NC,), jnp.float32) ** block_scale(streams_of[1], (NC,), ((0, 64),), -0.2, 0.2)), 0.1, 0.85)
    direction = with_ends((jax.random.randint(streams_of[2], (NC,), 0, 2) < 1).astype(jnp.int32), jax.random.fold_in(streams_of[2], 1), 0, 1)
    couple = jnp.clip(jax.random.uniform(streams_of[3], (F, F), jnp.float32, -0.25, 0.25), -0.25, 0.25)
    obs_place = with_ends(jax.random.randint(streams_of[4], (NOBS,), 0, CELLS_DEV), jax.random.fold_in(streams_of[4], 1), 0, CELLS_DEV - 1).astype(jnp.int32)
    obs_field = with_ends(jax.random.randint(streams_of[5], (NOBS,), 0, F), jax.random.fold_in(streams_of[5], 1), 0, F - 1).astype(jnp.int32)
    obs_value = noise(streams_of[6], (NOBS,), 2.0, 8.0, ((0, 64),), jnp.float32)
    obs_sigma = jnp.clip(jnp.exp(math.log(5.0) - 2.3025851 * jax.random.uniform(streams_of[7], (NOBS,), jnp.float32) ** block_scale(streams_of[7], (NOBS,), ((0, 64),), -0.2, 0.2)), 0.5, 5.0)
    send_count = draw_send_count(jax.random.fold_in(streams_of[9], 71), 0)
    return dict(ensemble=ensemble, speed=speed, direction=direction, couple=couple, obs_place=obs_place, obs_field=obs_field, obs_value=obs_value, obs_sigma=obs_sigma, send_count=send_count)


DIFFUSION = 0.05

def advance(states, speed, toward_left, toward_right, couple):
    padded = jnp.pad(states, ((0, 0), (0, 0), (1, 1)))
    left_cells = padded[:, :, :-2]
    right_cells = padded[:, :, 2:]
    advanced = states + toward_left * left_cells + toward_right * right_cells - speed * states + DIFFUSION * (left_cells - 2.0 * states + right_cells)
    return advanced + jnp.einsum('fg,kgc->kfc', couple, advanced, precision=lax.Precision.HIGHEST)

def mixing_matrix(upper_factor, carried, members):
    mean_weights = jax.scipy.linalg.solve_triangular(upper_factor, carried, lower=False)
    identity = jnp.eye(members, dtype=jnp.float32)
    spread = math.sqrt(members - 1.0) * jax.scipy.linalg.solve_triangular(upper_factor, identity, lower=False)
    centering = identity - 1.0 / members
    shifted = jnp.dot(centering, mean_weights, precision=lax.Precision.HIGHEST)
    inner = jnp.dot(jnp.dot(centering, spread, precision=lax.Precision.HIGHEST), centering, precision=lax.Precision.HIGHEST)
    return 1.0 / members + shifted[:, None] + inner

def reference(ensemble, speed, direction, couple, obs_place, obs_field, obs_value, obs_sigma, send_count):
    flag_values = direction.astype(jnp.float32)
    toward_left = speed * flag_values
    toward_right = speed - toward_left
    states = ensemble
    for step_index in range(STEPS):
        states = advance(states, speed, toward_left, toward_right, couple)
    owner_ends = jnp.cumsum(send_count, axis=1)
    slot_ids = jnp.arange(OBS_DEV, dtype=jnp.int32)
    owner_of = lax.optimization_barrier(jnp.sum((owner_ends[:, :, None] <= slot_ids[None, None, :]).astype(jnp.int32), axis=1))
    global_cell = owner_of.reshape(-1) * CELLS_DEV + obs_place
    flat_states = states.reshape(K, F * NC)
    picked = jnp.take(flat_states, obs_field * NC + global_cell, axis=1)
    center = lax.optimization_barrier(jnp.mean(picked, axis=0))
    scaled_anomaly = (picked - center) / obs_sigma
    innovation = (obs_value - center) / obs_sigma
    gram = jnp.dot(scaled_anomaly, scaled_anomaly.T, precision=lax.Precision.HIGHEST) + (K - 1.0) * jnp.eye(K, dtype=jnp.float32)
    cross = jnp.dot(scaled_anomaly, innovation, precision=lax.Precision.HIGHEST)
    lower_factor = jnp.linalg.cholesky(gram)
    carried = jax.scipy.linalg.solve_triangular(lower_factor, cross, lower=True)
    mixing = mixing_matrix(lower_factor.T, carried, K)
    analysis = jnp.einsum('kj,kfc->jfc', mixing, states, precision=lax.Precision.HIGHEST)
    return (analysis, innovation)
```

```python
import math

import jax
import jax.numpy as jnp
from jax import lax
from jax.experimental import pallas as pl
from jax.experimental.pallas import tpu as pltpu
from jax.sharding import PartitionSpec as P

STEPS = 4
DIFFUSION = 0.05
F = 4
K = 64
KL = 32
CELLS = 1024
HALF = 16
F32 = jnp.float32
I32 = jnp.int32
HIGHEST = lax.Precision.HIGHEST


def lanes_of(table, index):
    return jnp.take_along_axis(table, index, axis=1, mode="promise_in_bounds")


def kernel(
    ens, speed, direction, couple, place, field, value, sigma, counts,
    out, innov_out,
    states, split, coef, halo_out, halo_in, edge,
    m0, m1, m2, m3, slots, starts_s, counts_s, picked, innov_s,
    n0, n1, n2, n3, part, gy, gz, gx, gc, mix, send, recv, local,
):
    cells = lax.axis_index("cells")
    core = lax.axis_index("members")
    x = cells % 4
    z = (cells // 4) % 4
    y = cells // 16
    left_id = (cells + 63) % 64
    right_id = (cells + 1) % 64
    axes = {"x": (x, 1), "z": (z, 4), "y": (y, 16)}

    def peer(axis, step):
        mine, stride = axes[axis]
        other = (mine + step) % 4
        return other, {"cells": cells + (other - mine) * stride, "members": core}

    barrier = pltpu.get_barrier_semaphore()
    for axis in ("x", "z", "y"):
        for step in (1, 2, 3):
            pl.semaphore_signal(barrier, inc=1, device_id=peer(axis, step)[1])
    pl.semaphore_signal(barrier, inc=1, device_id={"cells": cells, "members": 1 - core})
    pl.semaphore_signal(barrier, inc=1, device_id={"cells": left_id, "members": core})
    pl.semaphore_signal(barrier, inc=1, device_id={"cells": right_id, "members": core})

    used = [0, 0]
    sent = []

    def copy_to(src, dst, device):
        at = used[0]
        used[0] += 1
        made = pltpu.make_async_remote_copy(
            src_ref=src, dst_ref=dst, send_sem=send.at[at], recv_sem=recv.at[at], device_id=device
        )
        made.start()
        sent.append(made)
        return made

    def copy_here(src, dst):
        at = used[1]
        used[1] += 1
        made = pltpu.make_async_copy(src, dst, local.at[at])
        made.start()
        return made

    def arrive(copies):
        for made in copies[:-1]:
            made.wait_recv()
        copies[-1].wait()

    lane = lax.broadcasted_iota(I32, (8, 128), 1)
    sub = lax.broadcasted_iota(I32, (8, 128), 0)
    lane64 = lax.broadcasted_iota(I32, (8, 64), 1)
    sub64 = lax.broadcasted_iota(I32, (8, 64), 0)

    flat = (field[...] * CELLS + place[...]).astype(F32)
    inverse = 1.0 / sigma[...]
    tables = []
    for quantity in (flat, value[...], inverse):
        tables.append([
            jnp.broadcast_to(quantity[:, h * 128 : (h + 1) * 128], (8, 128)) for h in (0, 1)
        ])
    count_row = jnp.broadcast_to(counts[...], (8, 64))

    def start_and_count(owner):
        begin = jnp.sum(jnp.where(lane64 < owner, count_row, 0), axis=1, keepdims=True)
        number = jnp.sum(jnp.where(lane64 == owner, count_row, 0), axis=1, keepdims=True)
        return begin, number

    slot = lane % 16
    which = (lane // 16) % 4
    upper = lane >= 64
    for g in range(4):
        row = sub64 + 8 * g
        base = (row // 2) % 4 * 4 + row // 8 + (row % 2) * 32
        b0, c0 = start_and_count(base)
        b1, c1 = start_and_count(base + 16)
        begin = jnp.where(upper, b1, b0)
        number = jnp.where(upper, c1, c0)
        rank = slot + HALF * core
        position = begin + rank
        low = position & 127
        second = position >= 128
        found = jnp.zeros((8, 128), F32)
        for q in range(3):
            got = jnp.where(second, lanes_of(tables[q][1], low), lanes_of(tables[q][0], low))
            found = jnp.where(which == q, got, found)
        found = jnp.where(rank < number, found, 0.0)
        m0[g] = found.reshape(4, 2, 1, 128)
    for g in range(8):
        row = sub64 + 8 * g
        begin, number = start_and_count(row % 4 * 16 + (row // 4) % 4 * 4 + row // 16)
        starts_s[8 * g : 8 * g + 8, :] = jnp.broadcast_to(begin, (8, 128))
        counts_s[8 * g : 8 * g + 8, :] = jnp.broadcast_to(number, (8, 128))

    toward_left = speed[...] * direction[...].astype(F32)
    for side, first in ((0, 896), (1, 0)):
        turned = jnp.transpose(ens[:, first : first + 128])
        halo_out[side, 0:8, :] = turned[120:128, :] if side == 0 else turned[0:8, :]
        halo_out[side, 8:9, :] = speed[:, first : first + 128]
        halo_out[side, 9:10, :] = toward_left[:, first : first + 128]
        halo_out[side, 10:16, :] = jnp.zeros((6, 128), F32)

    pl.semaphore_wait(barrier, 12)

    halo = [
        copy_to(halo_out.at[0], halo_in.at[0], {"cells": right_id, "members": core}),
        copy_to(halo_out.at[1], halo_in.at[1], {"cells": left_id, "members": core}),
    ]

    def exchange(axis, src_of, dst):
        made = [copy_to(src_of(peer(axis, s)[0]), dst, peer(axis, s)[1]) for s in (1, 2, 3)]
        return made + [copy_here(src_of(axes[axis][0]), dst)]

    going = exchange("x", lambda o: m0.at[o], m1.at[x])

    speed_row = speed[...]
    coef[0, :, 0:CELLS] = jnp.broadcast_to(1.0 - 2.0 * DIFFUSION - speed_row, (8, CELLS))
    coef[1, :, 0:CELLS] = jnp.broadcast_to(toward_left + DIFFUSION, (8, CELLS))
    coef[2, :, 0:CELLS] = jnp.broadcast_to(speed_row - toward_left + DIFFUSION, (8, CELLS))

    arrive(going)
    going = exchange("z", lambda o: m1.at[:, o], m2.at[z])

    for made in halo:
        made.wait_recv()
    has_left = jnp.where(cells > 0, 1.0, 0.0).astype(F32)
    has_right = jnp.where(cells < 63, 1.0, 0.0).astype(F32)
    present = jnp.where(lane < 64, has_right, has_left)
    edge[0:8, :] = halo_in[1, 0:8, :] * has_right
    edge[8:120, :] = jnp.zeros((112, 128), F32)
    edge[120:128, :] = halo_in[0, 0:8, :] * has_left
    edge[...] = jnp.transpose(edge[...])
    edge_speed = jnp.where(lane < 64, halo_in[1, 8:9, :], halo_in[0, 8:9, :])
    edge_left = jnp.where(lane < 64, halo_in[1, 9:10, :], halo_in[0, 9:10, :])
    coef[0, :, CELLS:] = present * (1.0 - 2.0 * DIFFUSION - edge_speed)
    coef[1, :, CELLS:] = present * (edge_left + DIFFUSION)
    coef[2, :, CELLS:] = present * (edge_speed - edge_left + DIFFUSION)

    def advance(group, carry):
        rows = pl.multiple_of(group * 8, 8)
        now = [
            jnp.concatenate([ens[pl.ds(f * KL + rows, 8), :], edge[pl.ds(f * KL + rows, 8), :]], axis=1)
            for f in range(F)
        ]
        for _ in range(STEPS):
            moved = [
                coef[0] * u
                + coef[1] * pltpu.roll(u, 1, 1)
                + coef[2] * pltpu.roll(u, CELLS + 127, 1)
                for u in now
            ]
            now = [
                moved[f] + sum(couple[f, g] * moved[g] for g in range(F)) for f in range(F)
            ]
        for f in range(F):
            states[f, pl.ds(pl.multiple_of(core * KL + rows, 8), 8), :] = now[f][:, 0:CELLS]
        return carry

    lax.fori_loop(0, 4, advance, 0)

    mine = states.at[:, pl.ds(pl.multiple_of(core * KL, KL), KL), :]
    swap = copy_to(mine, mine, {"cells": cells, "members": 1 - core})

    arrive(going)
    going = exchange("y", lambda o: m2.at[:, :, o // 2], m3.at[y])
    arrive(going)

    off = (y % 2) * 64
    for r in range(8):
        rows = m3[r // 2, 2 * (r % 2) : 2 * (r % 2) + 2].reshape(8, 128)
        for q in range(3):
            got = lanes_of(rows, off + 16 * q + slot)
            got = jnp.where(lane // 16 == sub, got, 0.0)
            slots[q, r : r + 1, :] = jnp.sum(got, axis=0, keepdims=True)

    swap.wait_recv()

    def pick(r, carry):
        index = jnp.broadcast_to(slots[0, pl.ds(r, 1), :], (8, 128)).astype(I32)
        low = index & 127
        high = index // 128
        found = [jnp.zeros((8, 128), F32)] * 8
        for c in range(32):
            here = high == c
            for g in range(8):
                tile = states[c // 8, 8 * g : 8 * g + 8, (c % 8) * 128 : (c % 8) * 128 + 128]
                found[g] = jnp.where(here, lanes_of(tile, low), found[g])
        total = found[0]
        for g in range(1, 8):
            total = total + found[g]
        center = jnp.sum(total, axis=0, keepdims=True) / K
        scale = slots[2, pl.ds(r, 1), :]
        at = pl.ds(pl.multiple_of(r * 128, 128), 128)
        for g in range(8):
            picked[8 * g : 8 * g + 8, at] = (found[g] - center) * scale
        row = (slots[1, pl.ds(r, 1), :] - center) * scale
        innov_s[:, at] = jnp.where(sub == 0, row, 0.0)
        n0[r] = row
        return carry

    lax.fori_loop(0, 8, pick, 0)

    contract = (((1,), (1,)), ((), ()))
    anomalies = picked[...]
    gram = lax.dot_general(anomalies, anomalies, contract, precision=HIGHEST, preferred_element_type=F32)
    cross = lax.dot_general(innov_s[...], anomalies, contract, precision=HIGHEST, preferred_element_type=F32)
    gy[y, 0:32, :] = jnp.concatenate([gram[0:32], gram[32:64]], axis=1)
    gy[y, 32:40, :] = jnp.concatenate([cross, jnp.zeros((8, 64), F32)], axis=1)

    def share(axis, ref):
        at = axes[axis][0]
        return [copy_to(ref.at[at], ref.at[at], peer(axis, s)[1]) for s in (1, 2, 3)]

    def collect(copies, ref):
        for made in copies:
            made.wait_recv()
        return (ref[0] + ref[1]) + (ref[2] + ref[3])

    adding = share("y", gy)
    back = exchange("y", lambda o: n0.at[pl.ds(2 * o, 2)], n1.at[y])

    for f in range(F):
        full = states[f]
        head = full.astype(jnp.bfloat16)
        split[f, 0:K, :] = head
        split[f, K : 2 * K, :] = (full - head.astype(F32)).astype(jnp.bfloat16)

    gz[z] = collect(adding, gy)
    adding = share("z", gz)
    arrive(back)
    back = exchange("z", lambda o: n1.at[:, o // 2], n2.at[z])

    gx[x] = collect(adding, gz)
    adding = share("x", gx)
    arrive(back)
    back = exchange("x", lambda o: n2, n3.at[x])

    gc[core] = collect(adding, gx)
    adding = copy_to(gc.at[core], gc.at[core], {"cells": cells, "members": 1 - core})

    arrive(back)
    shift = 64 * (z % 2) + 16 * x - HALF * core
    totals = [jnp.zeros((8, 128), F32)] * 2
    for g in range(8):
        rows = n3[g // 2, 2 * (g % 2) : 2 * (g % 2) + 2].reshape(8, 128)
        begin = starts_s[8 * g : 8 * g + 8, :]
        number = counts_s[8 * g : 8 * g + 8, :]
        for t in range(2):
            rank = lane + 128 * t - begin
            inside = rank - HALF * core
            good = (inside >= 0) & (inside < HALF) & (rank < number)
            got = lanes_of(rows, (rank + shift) & 127)
            totals[t] = totals[t] + jnp.where(good, got, 0.0)
    for t in range(2):
        part[core, t] = jnp.sum(totals[t], axis=0, keepdims=True)
    joined = copy_to(part.at[core], part.at[core], {"cells": cells, "members": 1 - core})

    adding.wait_recv()
    total = gc[0] + gc[1]

    a = []
    for h in range(8):
        packed = total[8 * (h % 4) : 8 * (h % 4) + 8]
        packed = packed if h < 4 else pltpu.roll(packed, 64, 1)
        packed = jnp.where(lane == sub + 8 * h, packed + (K - 1.0), packed)
        a.append(jnp.where(lane < K, packed, 0.0))
    pivots = [jnp.ones((8, 128), F32)] * 8
    for k in range(K):
        g, i = k // 8, k % 8
        at_k = lane == k
        row = jnp.broadcast_to(a[g][i : i + 1, :], (8, 128))
        pivot = jnp.broadcast_to(row[:, k : k + 1], (8, 128))
        over = 1.0 / pivot
        unit = jnp.where(at_k, 1.0, row)
        pivots[g] = jnp.where(sub == i, pivot, pivots[g])
        for h in range(g, 8):
            factor = jnp.broadcast_to(a[h][:, k : k + 1], (8, 128)) * over
            if h == g:
                factor = jnp.where(sub > i, factor, 0.0)
                kept = jnp.where(at_k & (sub > i), 0.0, a[h])
            else:
                kept = jnp.where(at_k, 0.0, a[h])
            a[h] = kept - factor * unit
    inv = []
    for h in range(8):
        row_id = sub + 8 * h
        unit = jnp.where(lane < row_id, a[h], jnp.where(lane == row_id, 1.0, 0.0))
        inv.append(unit / jnp.sqrt(pivots[h]))
    cross_row = jnp.where(lane[0:1] < K, total[32:33, :], 0.0)
    columns = jnp.zeros((8, 128), F32)
    weights = jnp.zeros((8, 128), F32)
    means = []
    for h in range(8):
        columns = columns + inv[h]
        means.append(jnp.sum(inv[h], axis=1, keepdims=True) / K)
        carried = jnp.sum(inv[h] * cross_row, axis=1, keepdims=True)
        weights = weights + inv[h] * carried
    column_mean = jnp.sum(columns, axis=0, keepdims=True) / K
    weight_row = jnp.sum(weights, axis=0, keepdims=True)
    grand = jnp.sum(column_mean, axis=1, keepdims=True) / K
    shifted = weight_row - jnp.sum(weight_row, axis=1, keepdims=True) / K + 1.0 / K
    for h in range(8):
        inner = inv[h] - means[h] - column_mean + grand
        rows = shifted + math.sqrt(K - 1.0) * inner
        mix[8 * h : 8 * h + 8, :] = jnp.where(lane < K, rows, pltpu.roll(rows, 64, 1))

    own = mix[pl.ds(pl.multiple_of(core * KL, KL), KL), :]
    head = own.astype(jnp.bfloat16)
    tail = (own - head.astype(F32)).astype(jnp.bfloat16)
    both = jnp.concatenate([head, tail], axis=0)
    for f in range(F):
        product = jnp.dot(both, split[f], preferred_element_type=F32)
        out[f] = product[0:KL] + product[KL : 2 * KL]

    joined.wait_recv()
    for t in range(2):
        innov_out[t : t + 1, :] = part[0, t] + part[1, t]
    for made in sent:
        made.wait_send()


def shards(
    ensemble, speed, direction, couple, obs_place, obs_field, obs_value, obs_sigma, send_count
):
    vmem = pl.BlockSpec(memory_space=pltpu.VMEM)
    smem = pl.BlockSpec(memory_space=pltpu.SMEM)
    row = lambda a: a.reshape(1, -1)
    by_field = jnp.transpose(ensemble, (1, 0, 2)).reshape(F * KL, CELLS)
    analysis, innovation = pl.pallas_call(
        kernel,
        out_shape=(
            jax.ShapeDtypeStruct((F, KL, CELLS), F32),
            jax.ShapeDtypeStruct((2, 128), F32),
        ),
        in_specs=[vmem, vmem, vmem, smem, vmem, vmem, vmem, vmem, vmem],
        out_specs=(vmem, vmem),
        scratch_shapes=[
            pltpu.VMEM((F, K, CELLS), F32),
            pltpu.VMEM((F, 2 * K, CELLS), jnp.bfloat16),
            pltpu.VMEM((3, 8, CELLS + 128), F32),
            pltpu.VMEM((2, 16, 128), F32),
            pltpu.VMEM((2, 16, 128), F32),
            pltpu.VMEM((128, 128), F32),
            pltpu.VMEM((4, 4, 2, 1, 128), F32),
            pltpu.VMEM((4, 4, 2, 1, 128), F32),
            pltpu.VMEM((4, 4, 2, 1, 128), F32),
            pltpu.VMEM((4, 4, 4, 1, 128), F32),
            pltpu.VMEM((3, 8, 128), F32),
            pltpu.VMEM((64, 128), I32),
            pltpu.VMEM((64, 128), I32),
            pltpu.VMEM((K, CELLS), F32),
            pltpu.VMEM((8, CELLS), F32),
            pltpu.VMEM((8, 1, 128), F32),
            pltpu.VMEM((4, 2, 1, 128), F32),
            pltpu.VMEM((4, 4, 1, 128), F32),
            pltpu.VMEM((4, 4, 4, 1, 128), F32),
            pltpu.VMEM((2, 2, 1, 128), F32),
            pltpu.VMEM((4, 40, 128), F32),
            pltpu.VMEM((4, 40, 128), F32),
            pltpu.VMEM((4, 40, 128), F32),
            pltpu.VMEM((2, 40, 128), F32),
            pltpu.VMEM((K, 128), F32),
            pltpu.SemaphoreType.DMA((32,)),
            pltpu.SemaphoreType.DMA((32,)),
            pltpu.SemaphoreType.DMA((6,)),
        ],
        compiler_params=pltpu.CompilerParams(collective_id=0, has_side_effects=True),
    )(
        by_field, row(speed), row(direction), couple, row(obs_place), row(obs_field),
        row(obs_value), row(obs_sigma), send_count,
    )
    return jnp.transpose(analysis, (1, 0, 2)), innovation.reshape(256)


def solution(mesh):
    return jax.shard_map(
        shards,
        mesh=mesh,
        in_specs=(
            P("members", None, "cells"),
            P("cells"),
            P("cells"),
            P(),
            P("cells"),
            P("cells"),
            P("cells"),
            P("cells"),
            P("cells", None),
        ),
        out_specs=(P("members", None, "cells"), P("cells")),
        check_vma=False,
    )
```

```python
import math

import jax
import jax.numpy as jnp
from jax import lax
from jax.experimental import pallas as pl
from jax.experimental.pallas import tpu as pltpu
from jax.sharding import PartitionSpec as P

STEPS = 4
DIFFUSION = 0.05
F = 4
K = 64
KL = 32
CELLS = 1024
HALF = 16
F32 = jnp.float32
I32 = jnp.int32
HIGHEST = lax.Precision.HIGHEST


def lanes_of(table, index):
    return jnp.take_along_axis(table, index, axis=1, mode="promise_in_bounds")


def kernel(
    ens_hbm, speed_hbm, direction_hbm, couple_hbm, place_hbm, field_hbm, value_hbm, sigma_hbm,
    counts_hbm, out_hbm, innov_out,
    ens, out, speed, direction, couple, place, field, value, sigma, counts,
    states, split, coef, halo_out, halo_in, edge,
    m0, m1, m2, m3, starts_s, counts_s, picked, innov_s,
    n0, n1, n2, n3, part, gy, gz, gx, gc, mix, send, recv, local, bulk,
):
    cells = lax.axis_index("cells")
    core = lax.axis_index("members")
    x = cells % 4
    z = (cells // 4) % 4
    y = cells // 16
    left_id = (cells + 63) % 64
    right_id = (cells + 1) % 64
    axes = {"x": (x, 1), "z": (z, 4), "y": (y, 16)}

    def peer(axis, step):
        mine, stride = axes[axis]
        other = (mine + step) % 4
        return other, {"cells": cells + (other - mine) * stride, "members": core}

    barrier = pltpu.get_barrier_semaphore()
    for axis in ("x", "z", "y"):
        for step in (1, 2, 3):
            pl.semaphore_signal(barrier, inc=1, device_id=peer(axis, step)[1])
    pl.semaphore_signal(barrier, inc=1, device_id={"cells": cells, "members": 1 - core})
    pl.semaphore_signal(barrier, inc=1, device_id={"cells": left_id, "members": core})
    pl.semaphore_signal(barrier, inc=1, device_id={"cells": right_id, "members": core})

    small = (
        (counts_hbm, counts), (place_hbm, place), (field_hbm, field), (value_hbm, value),
        (sigma_hbm, sigma), (speed_hbm, speed), (direction_hbm, direction), (couple_hbm, couple),
    )
    early = [pltpu.make_async_copy(src, dst, bulk.at[F + i]) for i, (src, dst) in enumerate(small)]
    loads = [
        pltpu.make_async_copy(ens_hbm.at[:, f], ens.at[pl.ds(f * KL, KL)], bulk.at[f]) for f in range(F)
    ]
    for made in early + loads:
        made.start()

    used = [0, 0]
    sent = []

    def copy_to(src, dst, device):
        at = used[0]
        used[0] += 1
        made = pltpu.make_async_remote_copy(
            src_ref=src, dst_ref=dst, send_sem=send.at[at], recv_sem=recv.at[at], device_id=device
        )
        made.start()
        sent.append(made)
        return made

    def copy_here(src, dst):
        at = used[1]
        used[1] += 1
        made = pltpu.make_async_copy(src, dst, local.at[at])
        made.start()
        return made

    def arrive(copies):
        for made in copies[:-1]:
            made.wait_recv()
        copies[-1].wait()

    lane = lax.broadcasted_iota(I32, (8, 128), 1)
    sub = lax.broadcasted_iota(I32, (8, 128), 0)
    lane64 = lax.broadcasted_iota(I32, (8, 64), 1)
    sub64 = lax.broadcasted_iota(I32, (8, 64), 0)

    for made in early:
        made.wait()
    flat = (field[...] * CELLS + place[...]).astype(F32)
    inverse = 1.0 / sigma[...]
    tables = []
    for quantity in (flat, value[...], inverse):
        tables.append([
            jnp.broadcast_to(quantity[:, h * 128 : (h + 1) * 128], (8, 128)) for h in (0, 1)
        ])
    count_row = jnp.broadcast_to(counts[...], (8, 64))

    def start_and_count(owner):
        begin = jnp.sum(jnp.where(lane64 < owner, count_row, 0), axis=1, keepdims=True)
        number = jnp.sum(jnp.where(lane64 == owner, count_row, 0), axis=1, keepdims=True)
        return begin, number

    slot = lane % 16
    which = (lane // 16) % 4
    upper = lane >= 64
    for g in range(4):
        row = sub64 + 8 * g
        base = (row // 2) % 4 * 4 + row // 8 + (row % 2) * 32
        b0, c0 = start_and_count(base)
        b1, c1 = start_and_count(base + 16)
        begin = jnp.where(upper, b1, b0)
        number = jnp.where(upper, c1, c0)
        rank = slot + HALF * core
        position = begin + rank
        low = position & 127
        second = position >= 128
        found = jnp.zeros((8, 128), F32)
        for q in range(3):
            got = jnp.where(second, lanes_of(tables[q][1], low), lanes_of(tables[q][0], low))
            found = jnp.where(which == q, got, found)
        found = jnp.where(rank < number, found, 0.0)
        m0[g] = found.reshape(4, 2, 1, 128)
    for g in range(8):
        row = sub64 + 8 * g
        begin, number = start_and_count(row % 4 * 16 + (row // 4) % 4 * 4 + row // 16)
        starts_s[8 * g : 8 * g + 8, :] = jnp.broadcast_to(begin, (8, 128))
        counts_s[8 * g : 8 * g + 8, :] = jnp.broadcast_to(number, (8, 128))

    for made in loads:
        made.wait()
    toward_left = speed[...] * direction[...].astype(F32)
    for side, first in ((0, 896), (1, 0)):
        turned = jnp.transpose(ens[:, first : first + 128])
        halo_out[side, 0:8, :] = turned[120:128, :] if side == 0 else turned[0:8, :]
        halo_out[side, 8:9, :] = speed[:, first : first + 128]
        halo_out[side, 9:10, :] = toward_left[:, first : first + 128]
        halo_out[side, 10:16, :] = jnp.zeros((6, 128), F32)

    pl.semaphore_wait(barrier, 12)

    halo = [
        copy_to(halo_out.at[0], halo_in.at[0], {"cells": right_id, "members": core}),
        copy_to(halo_out.at[1], halo_in.at[1], {"cells": left_id, "members": core}),
    ]

    def exchange(axis, src_of, dst):
        made = [copy_to(src_of(peer(axis, s)[0]), dst, peer(axis, s)[1]) for s in (1, 2, 3)]
        return made + [copy_here(src_of(axes[axis][0]), dst)]

    going = exchange("x", lambda o: m0.at[o], m1.at[x])

    gain = [[couple[f, g] + (1.0 if f == g else 0.0) for g in range(F)] for f in range(F)]
    for _ in range(2):
        gain = [
            [sum(gain[f][e] * gain[e][g] for e in range(F)) for g in range(F)] for f in range(F)
        ]
    speed_row = speed[...]
    coef[0, :, 0:CELLS] = jnp.broadcast_to(1.0 - 2.0 * DIFFUSION - speed_row, (8, CELLS))
    coef[1, :, 0:CELLS] = jnp.broadcast_to(toward_left + DIFFUSION, (8, CELLS))
    coef[2, :, 0:CELLS] = jnp.broadcast_to(speed_row - toward_left + DIFFUSION, (8, CELLS))

    def transport(u, centre, from_left, from_right):
        width = u.shape[1]
        for _ in range(STEPS):
            u = (
                centre * u
                + from_left * pltpu.roll(u, 1, 1)
                + from_right * pltpu.roll(u, width - 1, 1)
            )
        return u

    def coupled(moved):
        return [sum(gain[f][g] * moved[g] for g in range(F)) for f in range(F)]

    def interior(group, carry):
        rows = pl.multiple_of(group * 8, 8)
        into = pl.ds(pl.multiple_of(core * KL + rows, 8), 8)
        moved = [
            transport(
                ens[pl.ds(f * KL + rows, 8), :],
                coef[0, :, 0:CELLS], coef[1, :, 0:CELLS], coef[2, :, 0:CELLS],
            )
            for f in range(F)
        ]
        for f, made in enumerate(coupled(moved)):
            states[f, into, :] = made
        return carry

    lax.fori_loop(0, 4, interior, 0)

    arrive(going)
    going = exchange("z", lambda o: m1.at[:, o], m2.at[z])

    for made in halo:
        made.wait_recv()
    has_left = jnp.where(cells > 0, 1.0, 0.0).astype(F32)
    has_right = jnp.where(cells < 63, 1.0, 0.0).astype(F32)
    present = jnp.where(lane < 64, has_right, has_left)
    edge[0:8, :] = halo_in[1, 0:8, :] * has_right
    edge[8:120, :] = jnp.zeros((112, 128), F32)
    edge[120:128, :] = halo_in[0, 0:8, :] * has_left
    edge[...] = jnp.transpose(edge[...])
    edge_speed = jnp.where(lane < 64, halo_in[1, 8:9, :], halo_in[0, 8:9, :])
    edge_left = jnp.where(lane < 64, halo_in[1, 9:10, :], halo_in[0, 9:10, :])
    around = (
        present * (1.0 - 2.0 * DIFFUSION - edge_speed),
        present * (edge_left + DIFFUSION),
        present * (edge_speed - edge_left + DIFFUSION),
    )
    strip = [
        jnp.concatenate([coef[i, :, CELLS - 128 :], around[i], coef[i, :, 0:128]], axis=1)
        for i in range(3)
    ]

    def border(group, carry):
        rows = pl.multiple_of(group * 8, 8)
        into = pl.ds(pl.multiple_of(core * KL + rows, 8), 8)
        moved = []
        for f in range(F):
            at = pl.ds(f * KL + rows, 8)
            u = jnp.concatenate([ens[at, CELLS - 128 :], edge[at, :], ens[at, 0:128]], axis=1)
            moved.append(transport(u, *strip))
        for f, made in enumerate(coupled(moved)):
            before = states[f, into, CELLS - 128 :]
            states[f, into, CELLS - 128 :] = jnp.where(lane >= 64, made[:, 0:128], before)
            after = states[f, into, 0:128]
            states[f, into, 0:128] = jnp.where(lane < 64, made[:, 256:384], after)
        return carry

    lax.fori_loop(0, 4, border, 0)

    mine = states.at[:, pl.ds(pl.multiple_of(core * KL, KL), KL), :]
    swap = copy_to(mine, mine, {"cells": cells, "members": 1 - core})

    arrive(going)
    base = used[0]
    used[0] += 4
    own_rows = pltpu.make_async_copy(m2.at[:, :, y // 2], m3.at[y], recv.at[base])
    own_rows.start()
    for step in (1, 3, 2):
        o, device = peer("y", step)
        made = pltpu.make_async_remote_copy(
            src_ref=m2.at[:, :, o // 2], dst_ref=m3.at[y],
            send_sem=send.at[base + step], recv_sem=recv.at[base + step], device_id=device,
        )
        made.start()
        sent.append(made)
    swap.wait_recv()

    off = (y % 2) * 64

    def pick(turn, carry):
        t = turn // 2
        step = t + t // 2 - 2 * (t // 3)
        source = (y + 4 - step) % 4
        pair = turn % 2
        r = source * 2 + pair

        @pl.when(pair == 0)
        def _():
            pltpu.make_async_copy(m3.at[source], m3.at[source], recv.at[base + step]).wait()

        rows = m3[source, pl.ds(2 * pair, 2)].reshape(8, 128)
        asked = []
        for q in range(3):
            got = lanes_of(rows, off + 16 * q + slot)
            got = jnp.where(lane // 16 == sub, got, 0.0)
            asked.append(jnp.sum(got, axis=0, keepdims=True))
        index = jnp.broadcast_to(asked[0], (8, 128)).astype(I32)
        low = index & 127
        high = index // 128
        found = [jnp.zeros((8, 128), F32)] * 8
        for c in range(32):
            here = high == c
            for g in range(8):
                tile = states[c // 8, 8 * g : 8 * g + 8, (c % 8) * 128 : (c % 8) * 128 + 128]
                found[g] = jnp.where(here, lanes_of(tile, low), found[g])
        total = found[0]
        for g in range(1, 8):
            total = total + found[g]
        center = jnp.sum(total, axis=0, keepdims=True) / K
        at = pl.ds(pl.multiple_of(r * 128, 128), 128)
        for g in range(8):
            picked[8 * g : 8 * g + 8, at] = (found[g] - center) * asked[2]
        row = (asked[1] - center) * asked[2]
        innov_s[:, at] = jnp.where(sub == 0, row, 0.0)
        n0[r] = row
        return carry

    lax.fori_loop(0, 8, pick, 0)

    contract = (((1,), (1,)), ((), ()))
    anomalies = picked[...]
    gram = lax.dot_general(anomalies, anomalies, contract, precision=HIGHEST, preferred_element_type=F32)
    cross = lax.dot_general(innov_s[...], anomalies, contract, precision=HIGHEST, preferred_element_type=F32)
    gy[y, 0:32, :] = jnp.concatenate([gram[0:32], gram[32:64]], axis=1)
    gy[y, 32:40, :] = jnp.concatenate([cross, jnp.zeros((8, 64), F32)], axis=1)

    def share(axis, ref):
        at = axes[axis][0]
        return [copy_to(ref.at[at], ref.at[at], peer(axis, s)[1]) for s in (1, 2, 3)]

    def collect(copies, ref):
        for made in copies:
            made.wait_recv()
        return (ref[0] + ref[1]) + (ref[2] + ref[3])

    adding = share("y", gy)
    back = exchange("y", lambda o: n0.at[pl.ds(2 * o, 2)], n1.at[y])

    for f in range(F):
        full = states[f]
        head = full.astype(jnp.bfloat16)
        split[f, 0:K, :] = head
        split[f, K : 2 * K, :] = (full - head.astype(F32)).astype(jnp.bfloat16)

    gz[z] = collect(adding, gy)
    adding = share("z", gz)
    arrive(back)
    back = exchange("z", lambda o: n1.at[:, o // 2], n2.at[z])

    gx[x] = collect(adding, gz)
    adding = share("x", gx)
    arrive(back)
    back = exchange("x", lambda o: n2, n3.at[x])

    gc[core] = collect(adding, gx)
    adding = copy_to(gc.at[core], gc.at[core], {"cells": cells, "members": 1 - core})

    arrive(back)
    shift = 64 * (z % 2) + 16 * x - HALF * core
    totals = [jnp.zeros((8, 128), F32)] * 2
    for g in range(8):
        rows = n3[g // 2, 2 * (g % 2) : 2 * (g % 2) + 2].reshape(8, 128)
        begin = starts_s[8 * g : 8 * g + 8, :]
        number = counts_s[8 * g : 8 * g + 8, :]
        for t in range(2):
            rank = lane + 128 * t - begin
            inside = rank - HALF * core
            good = (inside >= 0) & (inside < HALF) & (rank < number)
            got = lanes_of(rows, (rank + shift) & 127)
            totals[t] = totals[t] + jnp.where(good, got, 0.0)
    for t in range(2):
        part[core, t] = jnp.sum(totals[t], axis=0, keepdims=True)
    joined = copy_to(part.at[core], part.at[core], {"cells": cells, "members": 1 - core})

    adding.wait_recv()
    total = gc[0] + gc[1]

    a = []
    for h in range(8):
        packed = total[8 * (h % 4) : 8 * (h % 4) + 8]
        packed = packed if h < 4 else pltpu.roll(packed, 64, 1)
        packed = jnp.where(lane == sub + 8 * h, packed + (K - 1.0), packed)
        a.append(jnp.where(lane < K, packed, 0.0))
    inv = []
    for g in range(8):
        first = 8 * g
        block = a[g]
        inside = (lane >= first) & (lane < first + 8)

        def column(rows, j):
            return jnp.broadcast_to(rows[:, first + j : first + j + 1], (8, 128))

        def spread_row(rows, i):
            return jnp.broadcast_to(rows[i : i + 1, :], (8, 128))

        columns = [column(block, j) for j in range(8)]
        d = {(i, j): spread_row(columns[j], i) for j in range(8) for i in range(j, 8)}
        over, low = [], {}
        for k in range(8):
            over.append(1.0 / d[k, k])
            for i in range(k + 1, 8):
                low[i, k] = d[i, k] * over[k]
            for j in range(k + 1, 8):
                for i in range(j, 8):
                    d[i, j] = d[i, j] - low[i, k] * d[j, k]
        m = {}
        for i in range(8):
            for j in range(i):
                total_ij = low[i, j]
                for e in range(j + 1, i):
                    total_ij = total_ij + low[i, e] * m[e, j]
                m[i, j] = -total_ij
        with_unit = jnp.where(inside, jnp.where(lane == sub + first, 1.0, 0.0), block)
        plain = [spread_row(with_unit, i) for i in range(8)]
        rows = []
        for i in range(8):
            made = plain[i]
            for e in range(i):
                made = made + m[i, e] * plain[e]
            rows.append(made)
        scaled = [rows[i] * over[i] for i in range(8)]
        solved = []
        for i in range(8):
            made = scaled[i]
            for e in range(i + 1, 8):
                made = made + m[e, i] * scaled[e]
            solved.append(made)
        for h in range(g + 1, 8):
            fresh = jnp.where(inside, 0.0, a[h])
            for i in range(8):
                fresh = fresh - column(a[h], i) * solved[i]
            a[h] = fresh
        final = jnp.zeros((8, 128), F32)
        for i in range(8):
            final = jnp.where(sub == i, rows[i] * jnp.sqrt(over[i]), final)
        inv.append(jnp.where(lane <= sub + first, final, 0.0))
    cross_row = jnp.where(lane[0:1] < K, total[32:33, :], 0.0)
    columns = jnp.zeros((8, 128), F32)
    weights = jnp.zeros((8, 128), F32)
    means = []
    for h in range(8):
        columns = columns + inv[h]
        means.append(jnp.sum(inv[h], axis=1, keepdims=True) / K)
        carried = jnp.sum(inv[h] * cross_row, axis=1, keepdims=True)
        weights = weights + inv[h] * carried
    column_mean = jnp.sum(columns, axis=0, keepdims=True) / K
    weight_row = jnp.sum(weights, axis=0, keepdims=True)
    grand = jnp.sum(column_mean, axis=1, keepdims=True) / K
    shifted = weight_row - jnp.sum(weight_row, axis=1, keepdims=True) / K + 1.0 / K
    for h in range(8):
        inner = inv[h] - means[h] - column_mean + grand
        rows = shifted + math.sqrt(K - 1.0) * inner
        mix[8 * h : 8 * h + 8, :] = jnp.where(lane < K, rows, pltpu.roll(rows, 64, 1))

    own = mix[pl.ds(pl.multiple_of(core * KL, KL), KL), :]
    head = own.astype(jnp.bfloat16)
    tail = (own - head.astype(F32)).astype(jnp.bfloat16)
    both = jnp.concatenate([head, tail], axis=0)
    stores = []
    for f in range(F):
        product = jnp.dot(both, split[f], preferred_element_type=F32)
        out[f] = product[0:KL] + product[KL : 2 * KL]
        stores.append(pltpu.make_async_copy(out.at[f], out_hbm.at[:, f], bulk.at[f]))
        stores[-1].start()

    joined.wait_recv()
    for t in range(2):
        innov_out[:, 128 * t : 128 * t + 128] = part[0, t] + part[1, t]
    for made in sent:
        made.wait_send()
    for made in stores:
        made.wait()


def shards(
    ensemble, speed, direction, couple, obs_place, obs_field, obs_value, obs_sigma, send_count
):
    vmem = pl.BlockSpec(memory_space=pltpu.VMEM)
    hbm = pl.BlockSpec(memory_space=pl.ANY)
    row = lambda a: a.reshape(1, -1)
    analysis, innovation = pl.pallas_call(
        kernel,
        out_shape=(
            jax.ShapeDtypeStruct((KL, F, CELLS), F32),
            jax.ShapeDtypeStruct((1, 256), F32),
        ),
        in_specs=[hbm] * 9,
        out_specs=(hbm, vmem),
        scratch_shapes=[
            pltpu.VMEM((F * KL, CELLS), F32),
            pltpu.VMEM((F, KL, CELLS), F32),
            pltpu.VMEM((1, CELLS), F32),
            pltpu.VMEM((1, CELLS), I32),
            pltpu.SMEM((F, F), F32),
            pltpu.VMEM((1, 256), I32),
            pltpu.VMEM((1, 256), I32),
            pltpu.VMEM((1, 256), F32),
            pltpu.VMEM((1, 256), F32),
            pltpu.VMEM((1, 64), I32),
            pltpu.VMEM((F, K, CELLS), F32),
            pltpu.VMEM((F, 2 * K, CELLS), jnp.bfloat16),
            pltpu.VMEM((3, 8, CELLS), F32),
            pltpu.VMEM((2, 16, 128), F32),
            pltpu.VMEM((2, 16, 128), F32),
            pltpu.VMEM((128, 128), F32),
            pltpu.VMEM((4, 4, 2, 1, 128), F32),
            pltpu.VMEM((4, 4, 2, 1, 128), F32),
            pltpu.VMEM((4, 4, 2, 1, 128), F32),
            pltpu.VMEM((4, 4, 4, 1, 128), F32),
            pltpu.VMEM((64, 128), I32),
            pltpu.VMEM((64, 128), I32),
            pltpu.VMEM((K, CELLS), F32),
            pltpu.VMEM((8, CELLS), F32),
            pltpu.VMEM((8, 1, 128), F32),
            pltpu.VMEM((4, 2, 1, 128), F32),
            pltpu.VMEM((4, 4, 1, 128), F32),
            pltpu.VMEM((4, 4, 4, 1, 128), F32),
            pltpu.VMEM((2, 2, 1, 128), F32),
            pltpu.VMEM((4, 40, 128), F32),
            pltpu.VMEM((4, 40, 128), F32),
            pltpu.VMEM((4, 40, 128), F32),
            pltpu.VMEM((2, 40, 128), F32),
            pltpu.VMEM((K, 128), F32),
            pltpu.SemaphoreType.DMA((33,)),
            pltpu.SemaphoreType.DMA((33,)),
            pltpu.SemaphoreType.DMA((6,)),
            pltpu.SemaphoreType.DMA((12,)),
        ],
        compiler_params=pltpu.CompilerParams(collective_id=0, has_side_effects=True),
    )(
        ensemble, row(speed), row(direction), couple, row(obs_place), row(obs_field),
        row(obs_value), row(obs_sigma), send_count,
    )
    return analysis, innovation.reshape(256)


def solution(mesh):
    return jax.shard_map(
        shards,
        mesh=mesh,
        in_specs=(
            P("members", None, "cells"),
            P("cells"),
            P("cells"),
            P(),
            P("cells"),
            P("cells"),
            P("cells"),
            P("cells"),
            P("cells", None),
        ),
        out_specs=(P("members", None, "cells"), P("cells")),
        check_vma=False,
    )
```

```python
import math

import jax
import jax.numpy as jnp
from jax import lax
from jax.experimental import pallas as pl
from jax.experimental.pallas import tpu as pltpu
from jax.sharding import PartitionSpec as P

STEPS = 4
DIFFUSION = 0.05
F = 4
K = 64
KL = 32
CELLS = 1024
FAR = (2, 1, 3, 0)
PLANE = [(dx, dz) for dx in FAR for dz in FAR]
AWAY = [(dx, dz, dy) for dy in FAR for dx, dz in PLANE if dx or dz or dy]
HALF = 16
F32 = jnp.float32
I32 = jnp.int32
HIGHEST = lax.Precision.HIGHEST


def lanes_of(table, index):
    return jnp.take_along_axis(table, index, axis=1, mode="promise_in_bounds")


def kernel(
    ens_hbm, speed_hbm, direction_hbm, couple_hbm, place_hbm, field_hbm, value_hbm, sigma_hbm,
    counts_hbm, out_hbm, innov_out,
    ens, out, speed, direction, couple, place, field, value, sigma, counts,
    states, split, coef, halo_out, halo_in, edge,
    m0, m3, starts_s, counts_s, picked, innov_s,
    n0, n3, part, gp, gy, gc, mix, send, recv, bulk,
    ask_send, ask_recv, back_send, back_recv, plane_send, plane_recv,
):
    cells = lax.axis_index("cells")
    core = lax.axis_index("members")
    x = lax.rem(cells, 4)
    z = lax.rem(cells // 4, 4)
    y = cells // 16
    left_id = lax.rem(cells + 63, 64)
    right_id = lax.rem(cells + 1, 64)
    pair_id = {"cells": cells, "members": 1 - core}
    xs = [lax.rem(x + d, 4) for d in range(4)]
    zs = [lax.rem(z + d, 4) for d in range(4)]
    ys = [lax.rem(y + d, 4) for d in range(4)]
    half_row = [t // 2 for t in ys]
    in_plane = {(dx, dz): zs[dz] * 4 + xs[dx] for dx, dz in PLANE}
    asked_row = {(dx, dz): xs[dx] * 8 + zs[dz] * 2 for dx, dz in PLANE}

    barrier = pltpu.get_barrier_semaphore()

    small = (
        (counts_hbm, counts), (place_hbm, place), (field_hbm, field), (value_hbm, value),
        (sigma_hbm, sigma), (speed_hbm, speed), (direction_hbm, direction), (couple_hbm, couple),
    )
    early = [pltpu.make_async_copy(src, dst, bulk.at[F + i]) for i, (src, dst) in enumerate(small)]
    loads = [
        pltpu.make_async_copy(ens_hbm.at[:, f], ens.at[pl.ds(f * KL, KL)], bulk.at[f]) for f in range(F)
    ]
    for made in early:
        made.start()
    for dx, dz, dy in AWAY:
        target = ys[dy] * 16 + in_plane[dx, dz]
        pl.semaphore_signal(barrier, inc=1, device_id={"cells": target, "members": core})
    pl.semaphore_signal(barrier, inc=1, device_id=pair_id)
    for made in loads:
        made.start()

    sent = []

    def copy_to(src, dst, at, device):
        made = pltpu.make_async_remote_copy(
            src_ref=src, dst_ref=dst, send_sem=send.at[at], recv_sem=recv.at[at], device_id=device
        )
        made.start()
        sent.append(made)
        return made

    def whole(ref, sem):
        return pltpu.make_async_copy(ref, ref, sem)

    lane = lax.broadcasted_iota(I32, (8, 128), 1)
    sub = lax.broadcasted_iota(I32, (8, 128), 0)
    lane64 = lax.broadcasted_iota(I32, (8, 64), 1)
    sub64 = lax.broadcasted_iota(I32, (8, 64), 0)

    for made in early:
        made.wait()
    flat = (field[...] * CELLS + place[...]).astype(F32)
    inverse = 1.0 / sigma[...]
    tables = []
    for quantity in (flat, value[...], inverse):
        tables.append([
            jnp.broadcast_to(quantity[:, h * 128 : (h + 1) * 128], (8, 128)) for h in (0, 1)
        ])
    count_row = jnp.broadcast_to(counts[...], (8, 64))

    def start_and_count(owner):
        begin = jnp.sum(jnp.where(lane64 < owner, count_row, 0), axis=1, keepdims=True)
        number = jnp.sum(jnp.where(lane64 == owner, count_row, 0), axis=1, keepdims=True)
        return begin, number

    slot = lane % 16
    which = (lane // 16) % 4
    upper = lane >= 64
    for g in range(4):
        row = sub64 + 8 * g
        base = (row // 2) % 4 * 4 + row // 8 + (row % 2) * 32
        b0, c0 = start_and_count(base)
        b1, c1 = start_and_count(base + 16)
        begin = jnp.where(upper, b1, b0)
        number = jnp.where(upper, c1, c0)
        rank = slot + HALF * core
        position = begin + rank
        low = position & 127
        second = position >= 128
        found = jnp.zeros((8, 128), F32)
        for q in range(3):
            got = jnp.where(second, lanes_of(tables[q][1], low), lanes_of(tables[q][0], low))
            found = jnp.where(which == q, got, found)
        found = jnp.where(rank < number, found, 0.0)
        m0[8 * g : 8 * g + 8] = found.reshape(8, 1, 128)
    for g in range(8):
        row = sub64 + 8 * g
        begin, number = start_and_count(row)
        starts_s[8 * g : 8 * g + 8, :] = jnp.broadcast_to(begin, (8, 128))
        counts_s[8 * g : 8 * g + 8, :] = jnp.broadcast_to(number, (8, 128))

    for made in loads:
        made.wait()
    toward_left = speed[...] * direction[...].astype(F32)
    for side, first in ((0, 896), (1, 0)):
        turned = jnp.transpose(ens[:, first : first + 128])
        halo_out[side, 0:8, :] = turned[120:128, :] if side == 0 else turned[0:8, :]
        halo_out[side, 8:9, :] = speed[:, first : first + 128]
        halo_out[side, 9:10, :] = toward_left[:, first : first + 128]
        halo_out[side, 10:16, :] = jnp.zeros((6, 128), F32)

    pl.semaphore_wait(barrier, 64)

    for dx, dz, dy in AWAY:
        target = ys[dy] * 16 + in_plane[dx, dz]
        pltpu.make_async_remote_copy(
            src_ref=m0.at[asked_row[dx, dz] + half_row[dy]], dst_ref=m3.at[cells],
            send_sem=ask_send.at[0], recv_sem=ask_recv.at[cells // 8],
            device_id={"cells": target, "members": core},
        ).start()
    own_row = asked_row[0, 0] + half_row[0]
    pltpu.make_async_copy(m0.at[own_row], m3.at[cells], ask_recv.at[cells // 8]).start()
    halo = [
        copy_to(halo_out.at[0], halo_in.at[0], 0, {"cells": right_id, "members": core}),
        copy_to(halo_out.at[1], halo_in.at[1], 1, {"cells": left_id, "members": core}),
    ]

    gain = [[couple[f, g] + (1.0 if f == g else 0.0) for g in range(F)] for f in range(F)]
    for _ in range(2):
        gain = [
            [sum(gain[f][e] * gain[e][g] for e in range(F)) for g in range(F)] for f in range(F)
        ]
    speed_row = speed[...]
    coef[0, :, 0:CELLS] = jnp.broadcast_to(1.0 - 2.0 * DIFFUSION - speed_row, (8, CELLS))
    coef[1, :, 0:CELLS] = jnp.broadcast_to(toward_left + DIFFUSION, (8, CELLS))
    coef[2, :, 0:CELLS] = jnp.broadcast_to(speed_row - toward_left + DIFFUSION, (8, CELLS))

    def transport(u, centre, from_left, from_right):
        width = u.shape[1]
        for _ in range(STEPS):
            u = (
                centre * u
                + from_left * pltpu.roll(u, 1, 1)
                + from_right * pltpu.roll(u, width - 1, 1)
            )
        return u

    def coupled(moved):
        return [sum(gain[f][g] * moved[g] for g in range(F)) for f in range(F)]

    def interior(group, carry):
        rows = pl.multiple_of(group * 8, 8)
        into = pl.ds(pl.multiple_of(core * KL + rows, 8), 8)
        moved = [
            transport(
                ens[pl.ds(f * KL + rows, 8), :],
                coef[0, :, 0:CELLS], coef[1, :, 0:CELLS], coef[2, :, 0:CELLS],
            )
            for f in range(F)
        ]
        for f, made in enumerate(coupled(moved)):
            states[f, into, :] = made
        return carry

    lax.fori_loop(0, 4, interior, 0)

    for made in halo:
        made.wait_recv()
    has_left = jnp.where(cells > 0, 1.0, 0.0).astype(F32)
    has_right = jnp.where(cells < 63, 1.0, 0.0).astype(F32)
    present = jnp.where(lane < 64, has_right, has_left)
    edge[0:8, :] = halo_in[1, 0:8, :] * has_right
    edge[8:120, :] = jnp.zeros((112, 128), F32)
    edge[120:128, :] = halo_in[0, 0:8, :] * has_left
    edge[...] = jnp.transpose(edge[...])
    edge_speed = jnp.where(lane < 64, halo_in[1, 8:9, :], halo_in[0, 8:9, :])
    edge_left = jnp.where(lane < 64, halo_in[1, 9:10, :], halo_in[0, 9:10, :])
    around = (
        present * (1.0 - 2.0 * DIFFUSION - edge_speed),
        present * (edge_left + DIFFUSION),
        present * (edge_speed - edge_left + DIFFUSION),
    )
    strip = [
        jnp.concatenate([coef[i, :, CELLS - 128 :], around[i], coef[i, :, 0:128]], axis=1)
        for i in range(3)
    ]

    def border(group, carry):
        rows = pl.multiple_of(group * 8, 8)
        into = pl.ds(pl.multiple_of(core * KL + rows, 8), 8)
        moved = []
        for f in range(F):
            at = pl.ds(f * KL + rows, 8)
            u = jnp.concatenate([ens[at, CELLS - 128 :], edge[at, :], ens[at, 0:128]], axis=1)
            moved.append(transport(u, *strip))
        for f, made in enumerate(coupled(moved)):
            before = states[f, into, CELLS - 128 :]
            states[f, into, CELLS - 128 :] = jnp.where(lane >= 64, made[:, 0:128], before)
            after = states[f, into, 0:128]
            states[f, into, 0:128] = jnp.where(lane < 64, made[:, 256:384], after)
        return carry

    lax.fori_loop(0, 4, border, 0)

    mine = states.at[:, pl.ds(pl.multiple_of(core * KL, KL), KL), :]
    swap = copy_to(mine, mine, 2, pair_id)

    swap.wait_recv()

    off = lax.rem(y, 2) * 64

    def answer(r):
        for i in range(8):
            source = 8 * r + i

            @pl.when(source != cells)
            def _():
                pltpu.make_async_remote_copy(
                    src_ref=n0.at[r], dst_ref=n3.at[cells], send_sem=back_send.at[0],
                    recv_sem=back_recv.at[0], device_id={"cells": source, "members": core},
                ).start()

            @pl.when(source == cells)
            def _():
                pltpu.make_async_copy(n0.at[r], n3.at[cells], back_recv.at[0]).start()

    def plane_at(t):
        step = t + t // 2 - 2 * (t // 3)
        return lax.rem(y + 4 - step, 4)

    def pick(t, carry):
        plane = plane_at(t)

        @pl.when(t > 0)
        def _():
            before = plane_at(t - 1)
            answer(2 * before)
            answer(2 * before + 1)

        asked = []
        for pair in range(2):
            r = 2 * plane + pair
            rows_ref = m3.at[pl.ds(8 * r, 8)]
            whole(rows_ref, ask_recv.at[r]).wait()
            rows = m3[pl.ds(8 * r, 8)].reshape(8, 128)
            for q in range(3):
                got = lanes_of(rows, off + 16 * q + slot)
                got = jnp.where(lane // 16 == sub, got, 0.0)
                asked.append(jnp.sum(got, axis=0, keepdims=True))
        for pair in range(2):
            r = 2 * plane + pair
            index, observed, scale = asked[3 * pair : 3 * pair + 3]
            index = jnp.broadcast_to(index, (8, 128)).astype(I32)
            low = index & 127
            high = index // 128
            found = [jnp.zeros((8, 128), F32)] * 8
            for c in range(32):
                here = high == c
                for g in range(8):
                    tile = states[c // 8, 8 * g : 8 * g + 8, (c % 8) * 128 : (c % 8) * 128 + 128]
                    found[g] = jnp.where(here, lanes_of(tile, low), found[g])
            total = found[0]
            for g in range(1, 8):
                total = total + found[g]
            center = jnp.sum(total, axis=0, keepdims=True) / K
            at = pl.ds(pl.multiple_of(r * 128, 128), 128)
            for g in range(8):
                picked[8 * g : 8 * g + 8, at] = (found[g] - center) * scale
            row = (observed - center) * scale
            innov_s[:, at] = jnp.where(sub == 0, row, 0.0)
            n0[r] = row
        return carry

    lax.fori_loop(0, 4, pick, 0)

    contract = (((1,), (1,)), ((), ()))
    anomalies = picked[...]
    gram = lax.dot_general(anomalies, anomalies, contract, precision=HIGHEST, preferred_element_type=F32)
    cross = lax.dot_general(innov_s[...], anomalies, contract, precision=HIGHEST, preferred_element_type=F32)
    here = z * 4 + x
    gp[here, 0:32, :] = jnp.concatenate([gram[0:32], gram[32:64]], axis=1)
    gp[here, 32:40, :] = jnp.concatenate([cross, jnp.zeros((8, 64), F32)], axis=1)

    for dx, dz in PLANE[:-1]:
        target = y * 16 + in_plane[dx, dz]
        pltpu.make_async_remote_copy(
            src_ref=gp.at[here], dst_ref=gp.at[here], send_sem=plane_send.at[0],
            recv_sem=plane_recv.at[0], device_id={"cells": target, "members": core},
        ).start()
    last = plane_at(3)
    answer(2 * last)
    answer(2 * last + 1)

    for f in range(F):
        full = states[f]
        head = full.astype(jnp.bfloat16)
        split[f, 0:K, :] = head
        split[f, K : 2 * K, :] = (full - head.astype(F32)).astype(jnp.bfloat16)

    whole(gp.at[pl.ds(0, 15)], plane_recv.at[0]).wait()
    total = gp[0]
    for i in range(1, 16):
        total = total + gp[i]
    gy[y] = total
    adding = [
        copy_to(gy.at[y], gy.at[y], 3 + step, {"cells": ys[step] * 16 + here, "members": core})
        for step in (2, 1, 3)
    ]
    for made in adding:
        made.wait_recv()
    gc[core] = (gy[0] + gy[1]) + (gy[2] + gy[3])
    adding = copy_to(gc.at[core], gc.at[core], 3, pair_id)

    whole(n3, back_recv.at[0]).wait()
    shift = 16 * lax.rem(cells, 8) - HALF * core
    totals = [jnp.zeros((8, 128), F32)] * 2
    for g in range(8):
        rows = n3[8 * g : 8 * g + 8].reshape(8, 128)
        begin = starts_s[8 * g : 8 * g + 8, :]
        number = counts_s[8 * g : 8 * g + 8, :]
        for t in range(2):
            rank = lane + 128 * t - begin
            inside = rank - HALF * core
            good = (inside >= 0) & (inside < HALF) & (rank < number)
            got = lanes_of(rows, (rank + shift) & 127)
            totals[t] = totals[t] + jnp.where(good, got, 0.0)
    for t in range(2):
        part[core, t] = jnp.sum(totals[t], axis=0, keepdims=True)
    joined = copy_to(part.at[core], part.at[core], 7, pair_id)

    adding.wait_recv()
    total = gc[0] + gc[1]

    a = []
    for h in range(8):
        packed = total[8 * (h % 4) : 8 * (h % 4) + 8]
        packed = packed if h < 4 else pltpu.roll(packed, 64, 1)
        packed = jnp.where(lane == sub + 8 * h, packed + (K - 1.0), packed)
        a.append(jnp.where(lane < K, packed, 0.0))
    inv = []
    for g in range(8):
        first = 8 * g
        block = a[g]
        inside = (lane >= first) & (lane < first + 8)

        def column(rows, j):
            return jnp.broadcast_to(rows[:, first + j : first + j + 1], (8, 128))

        def spread_row(rows, i):
            return jnp.broadcast_to(rows[i : i + 1, :], (8, 128))

        columns = [column(block, j) for j in range(8)]
        d = {(i, j): spread_row(columns[j], i) for j in range(8) for i in range(j, 8)}
        over, low = [], {}
        for k in range(8):
            over.append(1.0 / d[k, k])
            for i in range(k + 1, 8):
                low[i, k] = d[i, k] * over[k]
            for j in range(k + 1, 8):
                for i in range(j, 8):
                    d[i, j] = d[i, j] - low[i, k] * d[j, k]
        m = {}
        for i in range(8):
            for j in range(i):
                total_ij = low[i, j]
                for e in range(j + 1, i):
                    total_ij = total_ij + low[i, e] * m[e, j]
                m[i, j] = -total_ij
        with_unit = jnp.where(inside, jnp.where(lane == sub + first, 1.0, 0.0), block)
        plain = [spread_row(with_unit, i) for i in range(8)]
        rows = []
        for i in range(8):
            made = plain[i]
            for e in range(i):
                made = made + m[i, e] * plain[e]
            rows.append(made)
        scaled = [rows[i] * over[i] for i in range(8)]
        solved = []
        for i in range(8):
            made = scaled[i]
            for e in range(i + 1, 8):
                made = made + m[e, i] * scaled[e]
            solved.append(made)
        for h in range(g + 1, 8):
            fresh = jnp.where(inside, 0.0, a[h])
            for i in range(8):
                fresh = fresh - column(a[h], i) * solved[i]
            a[h] = fresh
        final = jnp.zeros((8, 128), F32)
        for i in range(8):
            final = jnp.where(sub == i, rows[i] * jnp.sqrt(over[i]), final)
        inv.append(jnp.where(lane <= sub + first, final, 0.0))
    cross_row = jnp.where(lane[0:1] < K, total[32:33, :], 0.0)
    columns = jnp.zeros((8, 128), F32)
    weights = jnp.zeros((8, 128), F32)
    means = []
    for h in range(8):
        columns = columns + inv[h]
        means.append(jnp.sum(inv[h], axis=1, keepdims=True) / K)
        carried = jnp.sum(inv[h] * cross_row, axis=1, keepdims=True)
        weights = weights + inv[h] * carried
    column_mean = jnp.sum(columns, axis=0, keepdims=True) / K
    weight_row = jnp.sum(weights, axis=0, keepdims=True)
    grand = jnp.sum(column_mean, axis=1, keepdims=True) / K
    shifted = weight_row - jnp.sum(weight_row, axis=1, keepdims=True) / K + 1.0 / K
    for h in range(8):
        inner = inv[h] - means[h] - column_mean + grand
        rows = shifted + math.sqrt(K - 1.0) * inner
        mix[8 * h : 8 * h + 8, :] = jnp.where(lane < K, rows, pltpu.roll(rows, 64, 1))

    own = mix[pl.ds(pl.multiple_of(core * KL, KL), KL), :]
    head = own.astype(jnp.bfloat16)
    tail = (own - head.astype(F32)).astype(jnp.bfloat16)
    both = jnp.concatenate([head, tail], axis=0)
    stores = []
    for f in range(F):
        product = jnp.dot(both, split[f], preferred_element_type=F32)
        out[f] = product[0:KL] + product[KL : 2 * KL]
        stores.append(pltpu.make_async_copy(out.at[f], out_hbm.at[:, f], bulk.at[f]))
        stores[-1].start()

    joined.wait_recv()
    for t in range(2):
        innov_out[:, 128 * t : 128 * t + 128] = part[0, t] + part[1, t]
    for made in sent:
        made.wait_send()
    for ref, sem in (
        (m3.at[pl.ds(0, 63)], ask_send), (n3.at[pl.ds(0, 63)], back_send), (gp.at[pl.ds(0, 15)], plane_send),
    ):
        whole(ref, sem.at[0]).wait()
    for made in stores:
        made.wait()


def shards(
    ensemble, speed, direction, couple, obs_place, obs_field, obs_value, obs_sigma, send_count
):
    vmem = pl.BlockSpec(memory_space=pltpu.VMEM)
    hbm = pl.BlockSpec(memory_space=pl.ANY)
    row = lambda a: a.reshape(1, -1)
    analysis, innovation = pl.pallas_call(
        kernel,
        out_shape=(
            jax.ShapeDtypeStruct((KL, F, CELLS), F32),
            jax.ShapeDtypeStruct((1, 256), F32),
        ),
        in_specs=[hbm] * 9,
        out_specs=(hbm, vmem),
        scratch_shapes=[
            pltpu.VMEM((F * KL, CELLS), F32),
            pltpu.VMEM((F, KL, CELLS), F32),
            pltpu.VMEM((1, CELLS), F32),
            pltpu.VMEM((1, CELLS), I32),
            pltpu.SMEM((F, F), F32),
            pltpu.VMEM((1, 256), I32),
            pltpu.VMEM((1, 256), I32),
            pltpu.VMEM((1, 256), F32),
            pltpu.VMEM((1, 256), F32),
            pltpu.VMEM((1, 64), I32),
            pltpu.VMEM((F, K, CELLS), F32),
            pltpu.VMEM((F, 2 * K, CELLS), jnp.bfloat16),
            pltpu.VMEM((3, 8, CELLS), F32),
            pltpu.VMEM((2, 16, 128), F32),
            pltpu.VMEM((2, 16, 128), F32),
            pltpu.VMEM((128, 128), F32),
            pltpu.VMEM((32, 1, 128), F32),
            pltpu.VMEM((64, 1, 128), F32),
            pltpu.VMEM((64, 128), I32),
            pltpu.VMEM((64, 128), I32),
            pltpu.VMEM((K, CELLS), F32),
            pltpu.VMEM((8, CELLS), F32),
            pltpu.VMEM((8, 1, 128), F32),
            pltpu.VMEM((64, 1, 128), F32),
            pltpu.VMEM((2, 2, 1, 128), F32),
            pltpu.VMEM((16, 40, 128), F32),
            pltpu.VMEM((4, 40, 128), F32),
            pltpu.VMEM((2, 40, 128), F32),
            pltpu.VMEM((K, 128), F32),
            pltpu.SemaphoreType.DMA((8,)),
            pltpu.SemaphoreType.DMA((8,)),
            pltpu.SemaphoreType.DMA((12,)),
            pltpu.SemaphoreType.DMA((1,)),
            pltpu.SemaphoreType.DMA((8,)),
            pltpu.SemaphoreType.DMA((1,)),
            pltpu.SemaphoreType.DMA((1,)),
            pltpu.SemaphoreType.DMA((1,)),
            pltpu.SemaphoreType.DMA((1,)),
        ],
        compiler_params=pltpu.CompilerParams(collective_id=0, has_side_effects=True),
    )(
        ensemble, row(speed), row(direction), couple, row(obs_place), row(obs_field),
        row(obs_value), row(obs_sigma), send_count,
    )
    return analysis, innovation.reshape(256)


def solution(mesh):
    return jax.shard_map(
        shards,
        mesh=mesh,
        in_specs=(
            P("members", None, "cells"),
            P("cells"),
            P("cells"),
            P(),
            P("cells"),
            P("cells"),
            P("cells"),
            P("cells"),
            P("cells", None),
        ),
        out_specs=(P("members", None, "cells"), P("cells")),
        check_vma=False,
    )
```

```python
import math

import jax
import jax.numpy as jnp
from jax import lax
from jax.experimental import pallas as pl
from jax.experimental.pallas import tpu as pltpu
from jax.sharding import PartitionSpec as P

STEPS = 4
DIFFUSION = 0.05
F = 4
K = 64
KL = 32
CELLS = 1024
FAR = (2, 1, 3, 0)
PLANE = [(dx, dz) for dx in FAR for dz in FAR]
AWAY = [(dx, dz, dy) for dy in FAR for dx, dz in PLANE if dx or dz or dy]
HALF = 16
F32 = jnp.float32
I32 = jnp.int32
HIGHEST = lax.Precision.HIGHEST


def lanes_of(table, index):
    return jnp.take_along_axis(table, index, axis=1, mode="promise_in_bounds")


def kernel(
    ens_hbm, speed_hbm, direction_hbm, couple_hbm, place_hbm, field_hbm, value_hbm, sigma_hbm,
    counts_hbm, out, innov_out,
    ens, speed, direction, couple, place, field, value, sigma, counts,
    states, split, coef, halo_out, halo_in, edge, base, keep, places, raw,
    m0, m3, starts_s, counts_s, gram_s, cross_s,
    n0, n3, part, g1, g2, gc, mix, send, recv, bulk,
    ask_send, ask_recv, back_send, back_recv, plane_send, plane_recv, halo_send, halo_recv,
):
    cells = lax.axis_index("cells")
    core = lax.axis_index("members")
    x = lax.rem(cells, 4)
    z = lax.rem(cells // 4, 4)
    y = cells // 16
    left_id = lax.rem(cells + 63, 64)
    right_id = lax.rem(cells + 1, 64)
    pair_id = {"cells": cells, "members": 1 - core}
    xs = [lax.rem(x + d, 4) for d in range(4)]
    zs = [lax.rem(z + d, 4) for d in range(4)]
    ys = [lax.rem(y + d, 4) for d in range(4)]
    half_row = [t // 2 for t in ys]
    in_plane = {(dx, dz): zs[dz] * 4 + xs[dx] for dx, dz in PLANE}
    asked_row = {(dx, dz): xs[dx] * 8 + zs[dz] * 2 for dx, dz in PLANE}

    barrier = pltpu.get_barrier_semaphore()

    for dx, dz, dy in AWAY:
        target = ys[dy] * 16 + in_plane[dx, dz]
        pl.semaphore_signal(barrier, inc=1, device_id={"cells": target, "members": core})
    pl.semaphore_signal(barrier, inc=1, device_id=pair_id)
    for neighbour in (left_id, right_id):
        pl.semaphore_signal(barrier, inc=1, device_id={"cells": neighbour, "members": 1 - core})
    small = (
        (counts_hbm, counts), (place_hbm, place), (field_hbm, field), (value_hbm, value),
        (sigma_hbm, sigma), (speed_hbm, speed), (direction_hbm, direction), (couple_hbm, couple),
    )
    early = [pltpu.make_async_copy(src, dst, bulk.at[F + i]) for i, (src, dst) in enumerate(small)]
    loads = [
        pltpu.make_async_copy(ens_hbm.at[:, f], ens.at[pl.ds(f * KL, KL)], bulk.at[f]) for f in range(F)
    ]
    for made in early:
        made.start()
    for made in loads:
        made.start()

    sent = []

    def copy_to(src, dst, at, device):
        made = pltpu.make_async_remote_copy(
            src_ref=src, dst_ref=dst, send_sem=send.at[at], recv_sem=recv.at[at], device_id=device
        )
        made.start()
        sent.append(made)
        return made

    def whole(ref, sem):
        return pltpu.make_async_copy(ref, ref, sem)

    lane = lax.broadcasted_iota(I32, (8, 128), 1)
    sub = lax.broadcasted_iota(I32, (8, 128), 0)
    lane64 = lax.broadcasted_iota(I32, (8, 64), 1)
    sub64 = lax.broadcasted_iota(I32, (8, 64), 0)

    for made in early:
        made.wait()
    flat = (field[...] * CELLS + place[...]).astype(F32)
    inverse = 1.0 / sigma[...]
    tables = []
    for quantity in (flat, value[...], inverse):
        tables.append([
            jnp.broadcast_to(quantity[:, h * 128 : (h + 1) * 128], (8, 128)) for h in (0, 1)
        ])
    count_row = jnp.broadcast_to(counts[...], (8, 64))

    def start_and_count(owner):
        begin = jnp.sum(jnp.where(lane64 < owner, count_row, 0), axis=1, keepdims=True)
        number = jnp.sum(jnp.where(lane64 == owner, count_row, 0), axis=1, keepdims=True)
        return begin, number

    slot = lane % 16
    which = (lane // 16) % 4
    upper = lane >= 64
    for g in range(4):
        row = sub64 + 8 * g
        lower = (row // 2) % 4 * 4 + row // 8 + (row % 2) * 32
        b0, c0 = start_and_count(lower)
        b1, c1 = start_and_count(lower + 16)
        begin = jnp.where(upper, b1, b0)
        number = jnp.where(upper, c1, c0)
        rank = slot + HALF * core
        position = begin + rank
        low = position & 127
        second = position >= 128
        found = jnp.zeros((8, 128), F32)
        for q in range(3):
            got = jnp.where(second, lanes_of(tables[q][1], low), lanes_of(tables[q][0], low))
            found = jnp.where(which == q, got, found)
        found = jnp.where(rank < number, found, 0.0)
        m0[8 * g : 8 * g + 8] = found.reshape(8, 1, 128)
    for g in range(8):
        row = sub64 + 8 * g
        begin, number = start_and_count(row)
        starts_s[8 * g : 8 * g + 8, :] = jnp.broadcast_to(begin, (8, 128))
        counts_s[8 * g : 8 * g + 8, :] = jnp.broadcast_to(number, (8, 128))

    for made in loads:
        made.wait()
    toward_left = speed[...] * direction[...].astype(F32)
    for side, first in ((0, 896), (1, 0)):
        turned = jnp.transpose(ens[:, first : first + 128])
        halo_out[side, 0:8, :] = turned[120:128, :] if side == 0 else turned[0:8, :]
        halo_out[side, 8:9, :] = speed[:, first : first + 128]
        halo_out[side, 9:10, :] = toward_left[:, first : first + 128]
        halo_out[side, 10:16, :] = jnp.zeros((6, 128), F32)
    wide = lax.broadcasted_iota(I32, (F * KL, 128), 1)
    base[core] = jnp.where(wide < 32, ens[:, 0:128], pltpu.roll(ens[:, CELLS - 128 :], 64, 1))

    for m in range(2):
        edge[m] = jnp.zeros((128, 128), F32)
    gram_s[...] = jnp.zeros((K, K), F32)
    cross_s[...] = jnp.zeros((K, 128), F32)
    keep[...] = jnp.zeros((2, 8, 128), F32)
    raw[...] = jnp.zeros((2, K, 256), F32)
    gain = [[couple[f, g] + (1.0 if f == g else 0.0) for g in range(F)] for f in range(F)]
    for _ in range(2):
        gain = [
            [sum(gain[f][e] * gain[e][g] for e in range(F)) for g in range(F)] for f in range(F)
        ]
    speed_row = speed[...]
    coef[0, :, 0:CELLS] = jnp.broadcast_to(1.0 - 2.0 * DIFFUSION - speed_row, (8, CELLS))
    coef[1, :, 0:CELLS] = jnp.broadcast_to(toward_left + DIFFUSION, (8, CELLS))
    coef[2, :, 0:CELLS] = jnp.broadcast_to(speed_row - toward_left + DIFFUSION, (8, CELLS))

    def transport(u, centre, from_left, from_right):
        width = u.shape[1]
        for _ in range(STEPS):
            u = (
                centre * u
                + from_left * pltpu.roll(u, 1, 1)
                + from_right * pltpu.roll(u, width - 1, 1)
            )
        return u

    def coupled(moved):
        return [sum(gain[f][g] * moved[g] for g in range(F)) for f in range(F)]

    def interior(group, carry):
        rows = pl.multiple_of(group * 8, 8)
        into = pl.ds(pl.multiple_of(core * KL + rows, 8), 8)
        moved = [
            transport(
                ens[pl.ds(f * KL + rows, 8), :],
                coef[0, :, 0:CELLS], coef[1, :, 0:CELLS], coef[2, :, 0:CELLS],
            )
            for f in range(F)
        ]
        for f, made in enumerate(coupled(moved)):
            states[f, into, :] = made
        return carry

    lax.fori_loop(0, 2, interior, 0)

    pl.semaphore_wait(barrier, 66)

    for to in range(2):
        for side, neighbour in ((0, right_id), (1, left_id)):
            pltpu.make_async_remote_copy(
                src_ref=halo_out.at[side], dst_ref=halo_in.at[side, core],
                send_sem=halo_send.at[0], recv_sem=halo_recv.at[0],
                device_id={"cells": neighbour, "members": to},
            ).start()
    based = copy_to(base.at[core], base.at[core], 0, pair_id)
    for dx, dz, dy in AWAY:
        target = ys[dy] * 16 + in_plane[dx, dz]
        pltpu.make_async_remote_copy(
            src_ref=m0.at[asked_row[dx, dz] + half_row[dy]], dst_ref=m3.at[cells],
            send_sem=ask_send.at[0], recv_sem=ask_recv.at[cells // 8],
            device_id={"cells": target, "members": core},
        ).start()
    own_row = asked_row[0, 0] + half_row[0]
    pltpu.make_async_copy(m0.at[own_row], m3.at[cells], ask_recv.at[cells // 8]).start()
    lax.fori_loop(2, 4, interior, 0)

    mine = states.at[:, pl.ds(pl.multiple_of(core * KL, KL), KL), :]
    swap = copy_to(mine, mine, 2, pair_id)

    based.wait_recv()
    whole(halo_in, halo_recv.at[0]).wait()
    swap.wait()
    has_left = jnp.where(cells > 0, 1.0, 0.0).astype(F32)
    has_right = jnp.where(cells < 63, 1.0, 0.0).astype(F32)
    for m in range(2):
        edge[m, 64:72, :] = halo_in[1, m, 0:8, :] * has_right
        edge[m, 120:128, :] = halo_in[0, m, 0:8, :] * has_left
        edge[m] = jnp.where(wide < 64, base[m], jnp.transpose(edge[m]))
    beyond = lane < 96
    present = jnp.where(beyond, has_right, has_left)

    def outside(row):
        after = jnp.broadcast_to(halo_in[1, 0, row : row + 1, :], (8, 128))
        before = jnp.broadcast_to(halo_in[0, 0, row : row + 1, :], (8, 128))
        return jnp.where(beyond, pltpu.roll(after, 64, 1), before)

    edge_speed, edge_left = outside(8), outside(9)
    around = (
        present * (1.0 - 2.0 * DIFFUSION - edge_speed),
        present * (edge_left + DIFFUSION),
        present * (edge_speed - edge_left + DIFFUSION),
    )
    strip = []
    for i in range(3):
        inner = jnp.where(lane < 32, coef[i, :, 0:128], pltpu.roll(coef[i, :, CELLS - 128 :], 64, 1))
        strip.append(jnp.where(lane < 64, inner, around[i]))

    def border(m, carry):
        for group in range(4):
            into = pl.ds(pl.multiple_of(m * KL + 8 * group, 8), 8)
            moved = [
                transport(edge[m, f * KL + 8 * group : f * KL + 8 * group + 8, :], *strip)
                for f in range(F)
            ]
            for f, made in enumerate(coupled(moved)):
                first = states[f, into, 0:128]
                states[f, into, 0:128] = jnp.where(lane < 4, made, first)
                last = states[f, into, CELLS - 128 :]
                states[f, into, CELLS - 128 :] = jnp.where(lane >= 124, pltpu.roll(made, 64, 1), last)
        return carry

    lax.fori_loop(0, 2, border, 0)

    off = lax.rem(y, 2) * 64

    def answer(r):
        for i in range(8):
            source = 8 * r + i

            @pl.when(source != cells)
            def _():
                pltpu.make_async_remote_copy(
                    src_ref=n0.at[r], dst_ref=n3.at[cells], send_sem=back_send.at[0],
                    recv_sem=back_recv.at[0], device_id={"cells": source, "members": core},
                ).start()

            @pl.when(source == cells)
            def _():
                pltpu.make_async_copy(n0.at[r], n3.at[cells], back_recv.at[0]).start()

    def plane_at(t):
        step = t + t // 2 - 2 * (t // 3)
        return lax.rem(y + 4 - step, 4)

    def finish(plane, turn):
        anomalies = [[] for _ in range(8)]
        crossed = [cross_s[8 * g : 8 * g + 8, :] for g in range(8)]
        for pair in range(2):
            r = 2 * plane + pair
            found = [raw[turn, 8 * g : 8 * g + 8, 128 * pair : 128 * pair + 128] for g in range(8)]
            total = found[0]
            for g in range(1, 8):
                total = total + found[g]
            center = jnp.sum(total, axis=0, keepdims=True) / K
            observed = keep[turn, pair : pair + 1, :]
            scale = keep[turn, 2 + pair : 3 + pair, :]
            row = (observed - center) * scale
            n0[r] = row
            for g in range(8):
                made = (found[g] - center) * scale
                anomalies[g].append(made)
                crossed[g] = crossed[g] + made * row
        stacked = jnp.concatenate([jnp.concatenate(a, axis=1) for a in anomalies], axis=0)
        gram_s[...] += lax.dot_general(
            stacked, stacked, (((1,), (1,)), ((), ())), precision=HIGHEST, preferred_element_type=F32
        )
        for g in range(8):
            cross_s[8 * g : 8 * g + 8, :] = crossed[g]

    def arrived(plane):
        for pair in range(2):
            r = 2 * plane + pair
            whole(m3.at[pl.ds(8 * r, 8)], ask_recv.at[r]).wait()

    def prepare(plane, turn):
        for pair in range(2):
            rows = m3[pl.ds(8 * (2 * plane + pair), 8)].reshape(8, 128)
            asked = []
            for q in range(3):
                got = lanes_of(rows, off + 16 * q + slot)
                got = jnp.where(lane // 16 == sub, got, 0.0)
                asked.append(jnp.sum(got, axis=0, keepdims=True))
            places[pair : pair + 1, :] = asked[0]
            keep[turn, pair : pair + 1, :] = asked[1]
            keep[turn, 2 + pair : 3 + pair, :] = asked[2]

    def pick(t, carry):
        turn = lax.rem(t, 2)

        @pl.when(t > 1)
        def _():
            before = plane_at(t - 2)
            answer(2 * before)
            answer(2 * before + 1)

        @pl.when(t < 3)
        def _():
            arrived(plane_at(t + 1))

        finish(plane_at(lax.rem(t + 3, 4)), 1 - turn)
        indices = [places[pair : pair + 1, :] for pair in range(2)]
        prepare(plane_at(lax.rem(t + 1, 4)), 1 - turn)
        for pair in range(2):
            index = jnp.broadcast_to(indices[pair], (8, 128)).astype(I32)
            low = index & 127
            high = index // 128
            found = [jnp.zeros((8, 128), F32)] * 8
            for c in range(32):
                here = high == c
                for g in range(8):
                    tile = states[c // 8, 8 * g : 8 * g + 8, (c % 8) * 128 : (c % 8) * 128 + 128]
                    found[g] = jnp.where(here, lanes_of(tile, low), found[g])
            for g in range(8):
                raw[turn, 8 * g : 8 * g + 8, 128 * pair : 128 * pair + 128] = found[g]
        return carry

    arrived(y)
    prepare(y, 0)
    lax.fori_loop(0, 4, pick, 0)
    finish(plane_at(3), 1)

    cross = jnp.sum(cross_s[...], axis=1, keepdims=True)
    gram = gram_s[...]
    apart = lax.broadcasted_iota(I32, (32, 64), 1)
    lower = jnp.where(
        apart >= 32, gram[32:64],
        jnp.where(apart == 0, cross[0:32], jnp.where(apart == 1, cross[32:64], 0.0)),
    )
    first_at = lax.rem(y, 2) * 4 + x
    g1[first_at] = jnp.concatenate([gram[0:32], lower], axis=1)

    beside = y + 1 - 2 * lax.rem(y, 2)
    for across, dx in ((1, 2), (0, 2), (1, 1), (1, 3), (0, 1), (0, 3), (1, 0)):
        target = (beside if across else y) * 16 + z * 4 + xs[dx]
        pltpu.make_async_remote_copy(
            src_ref=g1.at[first_at], dst_ref=g1.at[first_at], send_sem=plane_send.at[0],
            recv_sem=plane_recv.at[0], device_id={"cells": target, "members": core},
        ).start()
    for t in (2, 3):
        answer(2 * plane_at(t))
        answer(2 * plane_at(t) + 1)

    for f in range(F):
        full = states[f]
        head = full.astype(jnp.bfloat16)
        split[f, 0:K, :] = head
        split[f, K : 2 * K, :] = (full - head.astype(F32)).astype(jnp.bfloat16)

    whole(g1.at[pl.ds(0, 7)], plane_recv.at[0]).wait()

    def summed(ref):
        return ((ref[0] + ref[1]) + (ref[2] + ref[3])) + ((ref[4] + ref[5]) + (ref[6] + ref[7]))

    second_at = y // 2 * 4 + z
    g2[second_at] = summed(g1)
    for across, dz in ((1, 2), (0, 2), (1, 1), (1, 3), (0, 1), (0, 3), (1, 0)):
        target = (3 - y if across else y) * 16 + zs[dz] * 4 + x
        pltpu.make_async_remote_copy(
            src_ref=g2.at[second_at], dst_ref=g2.at[second_at], send_sem=plane_send.at[1],
            recv_sem=plane_recv.at[1], device_id={"cells": target, "members": core},
        ).start()
    whole(g2.at[pl.ds(0, 7)], plane_recv.at[1]).wait()
    gc[core] = summed(g2)
    adding = copy_to(gc.at[core], gc.at[core], 3, pair_id)

    whole(n3, back_recv.at[0]).wait()
    shift = 16 * lax.rem(cells, 8) - HALF * core
    totals = [jnp.zeros((8, 128), F32)] * 2
    for g in range(8):
        rows = n3[8 * g : 8 * g + 8].reshape(8, 128)
        begin = starts_s[8 * g : 8 * g + 8, :]
        number = counts_s[8 * g : 8 * g + 8, :]
        for t in range(2):
            rank = lane + 128 * t - begin
            inside = rank - HALF * core
            good = (inside >= 0) & (inside < HALF) & (rank < number)
            got = lanes_of(rows, (rank + shift) & 127)
            totals[t] = totals[t] + jnp.where(good, got, 0.0)
    for t in range(2):
        part[core, t] = jnp.sum(totals[t], axis=0, keepdims=True)
    joined = copy_to(part.at[core], part.at[core], 7, pair_id)

    adding.wait_recv()
    total = gc[0] + gc[1]

    turned = jnp.transpose(total)
    a = []
    for h in range(8):
        if h < 4:
            packed = total[8 * h : 8 * h + 8]
        else:
            left = jnp.concatenate([turned[8 * h : 8 * h + 8], jnp.zeros((8, 96), F32)], axis=1)
            right = pltpu.roll(total[8 * h - 32 : 8 * h - 24], 64, 1)
            packed = jnp.where(lane < 32, left, right)
        packed = jnp.where(lane == sub + 8 * h, packed + (K - 1.0), packed)
        a.append(jnp.where(lane < K, packed, 0.0))
    inv = []
    for g in range(8):
        first = 8 * g
        block = a[g]
        inside = (lane >= first) & (lane < first + 8)

        def column(rows, j):
            return jnp.broadcast_to(rows[:, first + j : first + j + 1], (8, 128))

        def spread_row(rows, i):
            return jnp.broadcast_to(rows[i : i + 1, :], (8, 128))

        columns = [column(block, j) for j in range(8)]
        d = {(i, j): spread_row(columns[j], i) for j in range(8) for i in range(j, 8)}
        over, low = [], {}
        for k in range(8):
            over.append(1.0 / d[k, k])
            for i in range(k + 1, 8):
                low[i, k] = d[i, k] * over[k]
            for j in range(k + 1, 8):
                for i in range(j, 8):
                    d[i, j] = d[i, j] - low[i, k] * d[j, k]
        m = {}
        for i in range(8):
            for j in range(i):
                total_ij = low[i, j]
                for e in range(j + 1, i):
                    total_ij = total_ij + low[i, e] * m[e, j]
                m[i, j] = -total_ij
        with_unit = jnp.where(inside, jnp.where(lane == sub + first, 1.0, 0.0), block)
        plain = [spread_row(with_unit, i) for i in range(8)]
        rows = []
        for i in range(8):
            made = plain[i]
            for e in range(i):
                made = made + m[i, e] * plain[e]
            rows.append(made)
        scaled = [rows[i] * over[i] for i in range(8)]
        solved = []
        for i in range(8):
            made = scaled[i]
            for e in range(i + 1, 8):
                made = made + m[e, i] * scaled[e]
            solved.append(made)
        for h in range(g + 1, 8):
            fresh = jnp.where(inside, 0.0, a[h])
            for i in range(8):
                fresh = fresh - column(a[h], i) * solved[i]
            a[h] = fresh
        final = jnp.zeros((8, 128), F32)
        for i in range(8):
            final = jnp.where(sub == i, rows[i] * jnp.sqrt(over[i]), final)
        inv.append(jnp.where(lane <= sub + first, final, 0.0))
    cross_row = jnp.concatenate([turned[64:65], turned[65:66], jnp.zeros((1, 64), F32)], axis=1)
    columns = jnp.zeros((8, 128), F32)
    weights = jnp.zeros((8, 128), F32)
    means = []
    for h in range(8):
        columns = columns + inv[h]
        means.append(jnp.sum(inv[h], axis=1, keepdims=True) / K)
        carried = jnp.sum(inv[h] * cross_row, axis=1, keepdims=True)
        weights = weights + inv[h] * carried
    column_mean = jnp.sum(columns, axis=0, keepdims=True) / K
    weight_row = jnp.sum(weights, axis=0, keepdims=True)
    grand = jnp.sum(column_mean, axis=1, keepdims=True) / K
    shifted = weight_row - jnp.sum(weight_row, axis=1, keepdims=True) / K + 1.0 / K
    for h in range(8):
        inner = inv[h] - means[h] - column_mean + grand
        rows = shifted + math.sqrt(K - 1.0) * inner
        mix[8 * h : 8 * h + 8, :] = jnp.where(lane < K, rows, pltpu.roll(rows, 64, 1))

    own = mix[pl.ds(pl.multiple_of(core * KL, KL), KL), :]
    head = own.astype(jnp.bfloat16)
    tail = (own - head.astype(F32)).astype(jnp.bfloat16)
    both = jnp.concatenate([head, tail], axis=0)
    for f in range(F):
        product = jnp.dot(both, split[f], preferred_element_type=F32)
        out[f] = product[0:KL] + product[KL : 2 * KL]

    joined.wait_recv()
    for t in range(2):
        innov_out[:, 128 * t : 128 * t + 128] = part[0, t] + part[1, t]
    for made in sent:
        if made is not swap:
            made.wait_send()
    for ref, sem in (
        (m3.at[pl.ds(0, 63)], ask_send), (n3.at[pl.ds(0, 63)], back_send), (halo_in, halo_send),
    ):
        whole(ref, sem.at[0]).wait()
    whole(g1.at[pl.ds(0, 7)], plane_send.at[0]).wait()
    whole(g2.at[pl.ds(0, 7)], plane_send.at[1]).wait()


def write_out(by_field, innovation, out_hbm, innov_hbm, sems):
    made = [pltpu.make_async_copy(innovation, innov_hbm, sems.at[F])]
    made += [pltpu.make_async_copy(by_field.at[f], out_hbm.at[:, f], sems.at[f]) for f in range(F)]
    for copy in made:
        copy.start()
    for copy in made:
        copy.wait()


def shards(
    ensemble, speed, direction, couple, obs_place, obs_field, obs_value, obs_sigma, send_count
):
    vmem = pl.BlockSpec(memory_space=pltpu.VMEM)
    hbm = pl.BlockSpec(memory_space=pl.ANY)
    row = lambda a: a.reshape(1, -1)
    analysis, innovation = pl.pallas_call(
        kernel,
        out_shape=(
            pltpu.VMEM((F, KL, CELLS), F32),
            pltpu.VMEM((1, 256), F32),
        ),
        in_specs=[hbm] * 9,
        out_specs=(vmem, vmem),
        scratch_shapes=[
            pltpu.VMEM((F * KL, CELLS), F32),
            pltpu.VMEM((1, CELLS), F32),
            pltpu.VMEM((1, CELLS), I32),
            pltpu.SMEM((F, F), F32),
            pltpu.VMEM((1, 256), I32),
            pltpu.VMEM((1, 256), I32),
            pltpu.VMEM((1, 256), F32),
            pltpu.VMEM((1, 256), F32),
            pltpu.VMEM((1, 64), I32),
            pltpu.VMEM((F, K, CELLS), F32),
            pltpu.VMEM((F, 2 * K, CELLS), jnp.bfloat16),
            pltpu.VMEM((3, 8, CELLS), F32),
            pltpu.VMEM((2, 16, 128), F32),
            pltpu.VMEM((2, 2, 16, 128), F32),
            pltpu.VMEM((2, 128, 128), F32),
            pltpu.VMEM((2, 128, 128), F32),
            pltpu.VMEM((2, 8, 128), F32),
            pltpu.VMEM((8, 128), F32),
            pltpu.VMEM((2, K, 256), F32),
            pltpu.VMEM((32, 1, 128), F32),
            pltpu.VMEM((64, 1, 128), F32),
            pltpu.VMEM((64, 128), I32),
            pltpu.VMEM((64, 128), I32),
            pltpu.VMEM((K, K), F32),
            pltpu.VMEM((K, 128), F32),
            pltpu.VMEM((8, 1, 128), F32),
            pltpu.VMEM((64, 1, 128), F32),
            pltpu.VMEM((2, 2, 1, 128), F32),
            pltpu.VMEM((8, 32, 128), F32),
            pltpu.VMEM((8, 32, 128), F32),
            pltpu.VMEM((2, 32, 128), F32),
            pltpu.VMEM((K, 128), F32),
            pltpu.SemaphoreType.DMA((8,)),
            pltpu.SemaphoreType.DMA((8,)),
            pltpu.SemaphoreType.DMA((12,)),
            pltpu.SemaphoreType.DMA((1,)),
            pltpu.SemaphoreType.DMA((8,)),
            pltpu.SemaphoreType.DMA((1,)),
            pltpu.SemaphoreType.DMA((1,)),
            pltpu.SemaphoreType.DMA((2,)),
            pltpu.SemaphoreType.DMA((2,)),
            pltpu.SemaphoreType.DMA((1,)),
            pltpu.SemaphoreType.DMA((1,)),
        ],
        compiler_params=pltpu.CompilerParams(collective_id=0, has_side_effects=True),
    )(
        ensemble, row(speed), row(direction), couple, row(obs_place), row(obs_field),
        row(obs_value), row(obs_sigma), send_count,
    )
    analysis, innovation = pl.pallas_call(
        write_out,
        out_shape=(
            jax.ShapeDtypeStruct((KL, F, CELLS), F32),
            jax.ShapeDtypeStruct((1, 256), F32),
        ),
        in_specs=[vmem, vmem],
        out_specs=(hbm, hbm),
        scratch_shapes=[pltpu.SemaphoreType.DMA((F + 1,))],
    )(*(pltpu.with_memory_space_constraint(a, pltpu.VMEM) for a in (analysis, innovation)))
    return analysis, innovation.reshape(256)


def solution(mesh):
    return jax.shard_map(
        shards,
        mesh=mesh,
        in_specs=(
            P("members", None, "cells"),
            P("cells"),
            P("cells"),
            P(),
            P("cells"),
            P("cells"),
            P("cells"),
            P("cells"),
            P("cells", None),
        ),
        out_specs=(P("members", None, "cells"), P("cells")),
        check_vma=False,
    )
```

```python
import math

import jax
import jax.numpy as jnp
from jax import lax
from jax.experimental import pallas as pl
from jax.experimental.pallas import tpu as pltpu
from jax.sharding import PartitionSpec as P

STEPS = 4
DIFFUSION = 0.05
F = 4
K = 64
KL = 32
CELLS = 1024
FAR = (2, 1, 3, 0)
PLANE = [(dx, dz) for dx in FAR for dz in FAR]
F32 = jnp.float32
I32 = jnp.int32
HIGHEST = lax.Precision.HIGHEST


def lanes_of(table, index):
    return jnp.take_along_axis(table, index, axis=1, mode="promise_in_bounds")


def kernel(
    ens_hbm, speed_hbm, direction_hbm, couple_hbm, place_hbm, field_hbm, value_hbm, sigma_hbm,
    counts_hbm, out, innov_out,
    ens, speed, direction, couple, place, field, value, sigma, counts,
    states, split, coef, halo_out, halo_in, edge, base, keep, places, raw,
    m0, m3, starts_s, counts_s, gram_s, cross_s,
    n0, n3, part, g1, g2, gc, e1, e2, ec, mix, send, recv, bulk,
    ask_send, ask_recv, back_send, back_recv, plane_send, plane_recv, halo_send, halo_recv,
):
    cells = lax.axis_index("cells")
    core = lax.axis_index("members")
    x = lax.rem(cells, 4)
    z = lax.rem(cells // 4, 4)
    y = cells // 16
    left_id = lax.rem(cells + 63, 64)
    right_id = lax.rem(cells + 1, 64)
    pair_id = {"cells": cells, "members": 1 - core}
    xs = [lax.rem(x + d, 4) for d in range(4)]
    zs = [lax.rem(z + d, 4) for d in range(4)]
    ys = [lax.rem(y + d, 4) for d in range(4)]
    parity = lax.rem(x, 2)
    in_plane = {(dx, dz): zs[dz] * 4 + xs[dx] for dx, dz in PLANE}
    own_ys = [lax.rem(y + core + 2 * i, 4) for i in range(2)]
    served_x = [lax.rem(x + lax.rem(x + core, 2) + 2 * i, 4) for i in range(2)]
    alone = core + parity == 0
    early_at = x + core * (z - x)
    late_at = z + core * (x - z)
    early_stride = 1 + 3 * core
    late_stride = 4 - 3 * core
    beside = y + 1 - 2 * lax.rem(y, 2)
    group1, group2 = [], []
    for across, step in ((1, 2), (0, 2), (1, 1), (1, 3), (0, 1), (0, 3), (1, 0)):
        along = lax.rem(early_at + step, 4) * early_stride + late_at * late_stride
        group1.append({"cells": (beside if across else y) * 16 + along, "members": core})
        along = lax.rem(late_at + step, 4) * late_stride + early_at * early_stride
        group2.append({"cells": (3 - y if across else y) * 16 + along, "members": core})
    asked_of = [
        (own_ys[i] * 16 + in_plane[dx, dz], i * 16 + in_plane[dx, dz], (dx, dz, i))
        for i in (1, 0) for dx, dz in PLANE
    ]

    barrier = pltpu.get_barrier_semaphore()

    for target, _, at in asked_of[:-1]:
        pl.semaphore_signal(barrier, inc=1, device_id={"cells": target, "members": parity})
    for dy in (2, 1, 3, 0):
        for dz in FAR:
            for i in (1, 0):
                if (dy, dz, i) != (0, 0, 0):
                    target = ys[dy] * 16 + zs[dz] * 4 + served_x[i]
                    pl.semaphore_signal(
                        barrier, inc=1, device_id={"cells": target, "members": dy % 2}
                    )
    for device in group1 + group2:
        pl.semaphore_signal(barrier, inc=1, device_id=device)
    @pl.when(jnp.logical_not(alone))
    def _():
        pl.semaphore_signal(
            barrier, inc=1, device_id={"cells": asked_of[-1][0], "members": parity}
        )

    @pl.when(jnp.logical_not(alone))
    def _():
        pl.semaphore_signal(
            barrier, inc=1, device_id={"cells": y * 16 + z * 4 + served_x[0], "members": 0}
        )

    pl.semaphore_signal(barrier, inc=1, device_id=pair_id)
    for neighbour in (left_id, right_id):
        for to in range(2):
            pl.semaphore_signal(barrier, inc=1, device_id={"cells": neighbour, "members": to})
    small = (
        (counts_hbm, counts), (place_hbm, place), (field_hbm, field), (value_hbm, value),
        (sigma_hbm, sigma), (speed_hbm, speed), (direction_hbm, direction), (couple_hbm, couple),
    )
    early = [pltpu.make_async_copy(src, dst, bulk.at[F + i]) for i, (src, dst) in enumerate(small)]
    loads = [
        pltpu.make_async_copy(ens_hbm.at[:, f], ens.at[pl.ds(f * KL, KL)], bulk.at[f]) for f in range(F)
    ]
    for made in early:
        made.start()
    for made in loads:
        made.start()

    sent = []

    def copy_to(src, dst, at, device):
        made = pltpu.make_async_remote_copy(
            src_ref=src, dst_ref=dst, send_sem=send.at[at], recv_sem=recv.at[at], device_id=device
        )
        made.start()
        sent.append(made)
        return made

    def whole(ref, sem):
        return pltpu.make_async_copy(ref, ref, sem)

    lane = lax.broadcasted_iota(I32, (8, 128), 1)
    sub = lax.broadcasted_iota(I32, (8, 128), 0)
    lane64 = lax.broadcasted_iota(I32, (8, 64), 1)
    sub64 = lax.broadcasted_iota(I32, (8, 64), 0)

    for made in early:
        made.wait()
    flat = (field[...] * CELLS + place[...]).astype(F32)
    inverse = 1.0 / sigma[...]
    tables = []
    for quantity in (flat, value[...], inverse):
        tables.append([
            jnp.broadcast_to(quantity[:, h * 128 : (h + 1) * 128], (8, 128)) for h in (0, 1)
        ])
    count_row = jnp.broadcast_to(counts[...], (8, 64))

    def start_and_count(owner):
        begin = jnp.sum(jnp.where(lane64 < owner, count_row, 0), axis=1, keepdims=True)
        number = jnp.sum(jnp.where(lane64 == owner, count_row, 0), axis=1, keepdims=True)
        return begin, number

    slot = lane % 32
    which = lane // 32
    for g in range(4):
        row = sub64 + 8 * g
        owner_y = own_ys[g // 2]
        begin, number = start_and_count(owner_y * 16 + row % 16)
        begin = jnp.broadcast_to(begin, (8, 128))
        number = jnp.broadcast_to(number, (8, 128))
        starts_s[8 * g : 8 * g + 8, :] = begin
        counts_s[8 * g : 8 * g + 8, :] = number
        position = begin + slot
        low = position & 127
        second = position >= 128
        found = jnp.zeros((8, 128), F32)
        for q in range(3):
            got = jnp.where(second, lanes_of(tables[q][1], low), lanes_of(tables[q][0], low))
            found = jnp.where(which == q, got, found)
        found = jnp.where(slot < number, found, 0.0)
        m0[8 * g : 8 * g + 8] = found.reshape(8, 1, 128)

    for made in loads:
        made.wait()
    toward_left = speed[...] * direction[...].astype(F32)
    for side, first in ((0, 896), (1, 0)):
        turned = jnp.transpose(ens[:, first : first + 128])
        halo_out[side, 0:8, :] = turned[120:128, :] if side == 0 else turned[0:8, :]
        halo_out[side, 8:9, :] = speed[:, first : first + 128]
        halo_out[side, 9:10, :] = toward_left[:, first : first + 128]
        halo_out[side, 10:16, :] = jnp.zeros((6, 128), F32)
    wide = lax.broadcasted_iota(I32, (F * KL, 128), 1)
    base[core] = jnp.where(wide < 32, ens[:, 0:128], pltpu.roll(ens[:, CELLS - 128 :], 64, 1))

    for m in range(2):
        edge[m] = jnp.zeros((128, 128), F32)
    gram_s[...] = jnp.zeros((K, K), F32)
    cross_s[...] = jnp.zeros((K, 128), F32)
    keep[...] = jnp.zeros((2, 8, 128), F32)
    raw[...] = jnp.zeros((2, K, 256), F32)
    gain = [[couple[f, g] + (1.0 if f == g else 0.0) for g in range(F)] for f in range(F)]
    for _ in range(2):
        gain = [
            [sum(gain[f][e] * gain[e][g] for e in range(F)) for g in range(F)] for f in range(F)
        ]
    speed_row = speed[...]
    coef[0, :, 0:CELLS] = jnp.broadcast_to(1.0 - 2.0 * DIFFUSION - speed_row, (8, CELLS))
    coef[1, :, 0:CELLS] = jnp.broadcast_to(toward_left + DIFFUSION, (8, CELLS))
    coef[2, :, 0:CELLS] = jnp.broadcast_to(speed_row - toward_left + DIFFUSION, (8, CELLS))

    def transport(u, centre, from_left, from_right):
        width = u.shape[1]
        for _ in range(STEPS):
            u = (
                centre * u
                + from_left * pltpu.roll(u, 1, 1)
                + from_right * pltpu.roll(u, width - 1, 1)
            )
        return u

    def coupled(moved):
        return [sum(gain[f][g] * moved[g] for g in range(F)) for f in range(F)]

    def interior(group, carry):
        rows = pl.multiple_of(group * 8, 8)
        into = pl.ds(pl.multiple_of(core * KL + rows, 8), 8)
        moved = [
            transport(
                ens[pl.ds(f * KL + rows, 8), :],
                coef[0, :, 0:CELLS], coef[1, :, 0:CELLS], coef[2, :, 0:CELLS],
            )
            for f in range(F)
        ]
        for f, made in enumerate(coupled(moved)):
            states[f, into, :] = made
        return carry

    lax.fori_loop(0, 2, interior, 0)

    pl.semaphore_wait(barrier, 83 - 2 * jnp.where(alone, 1, 0))

    sides = ((0, right_id, cells < 63, cells > 0), (1, left_id, cells > 0, cells < 63))
    for side, neighbour, sends, _ in sides:

        @pl.when(sends)
        def _():
            for to in range(2):
                pltpu.make_async_remote_copy(
                    src_ref=halo_out.at[side], dst_ref=halo_in.at[side, core],
                    send_sem=halo_send.at[side], recv_sem=halo_recv.at[side],
                    device_id={"cells": neighbour, "members": to},
                ).start()

        @pl.when(jnp.logical_not(sends))
        def _():
            halo_in[1 - side] = jnp.zeros((2, 16, 128), F32)

    based = copy_to(base.at[core], base.at[core], 0, pair_id)
    source_at = y * 8 + z * 2 + x // 2

    def ask(target, row):
        pltpu.make_async_remote_copy(
            src_ref=m0.at[row], dst_ref=m3.at[source_at], send_sem=ask_send.at[0],
            recv_sem=ask_recv.at[cells // 8], device_id={"cells": target, "members": parity},
        ).start()

    for target, row, at in asked_of[:-1]:
        ask(target, row)

    @pl.when(jnp.logical_not(alone))
    def _():
        ask(*asked_of[-1][:2])

    @pl.when(alone)
    def _():
        pltpu.make_async_copy(m0.at[asked_of[-1][1]], m3.at[source_at], ask_recv.at[cells // 8]).start()

    lax.fori_loop(2, 4, interior, 0)

    mine = states.at[:, pl.ds(pl.multiple_of(core * KL, KL), KL), :]
    swap = copy_to(mine, mine, 2, pair_id)

    based.wait_recv()
    for side, _, _, receives in sides:

        @pl.when(receives)
        def _():
            whole(halo_in.at[side], halo_recv.at[side]).wait()

    swap.wait()
    has_left = jnp.where(cells > 0, 1.0, 0.0).astype(F32)
    has_right = jnp.where(cells < 63, 1.0, 0.0).astype(F32)
    for m in range(2):
        edge[m, 64:72, :] = halo_in[1, m, 0:8, :] * has_right
        edge[m, 120:128, :] = halo_in[0, m, 0:8, :] * has_left
        edge[m] = jnp.where(wide < 64, base[m], jnp.transpose(edge[m]))
    beyond = lane < 96
    present = jnp.where(beyond, has_right, has_left)

    def outside(row):
        after = jnp.broadcast_to(halo_in[1, 0, row : row + 1, :], (8, 128))
        before = jnp.broadcast_to(halo_in[0, 0, row : row + 1, :], (8, 128))
        return jnp.where(beyond, pltpu.roll(after, 64, 1), before)

    edge_speed, edge_left = outside(8), outside(9)
    around = (
        present * (1.0 - 2.0 * DIFFUSION - edge_speed),
        present * (edge_left + DIFFUSION),
        present * (edge_speed - edge_left + DIFFUSION),
    )
    strip = []
    for i in range(3):
        inner = jnp.where(lane < 32, coef[i, :, 0:128], pltpu.roll(coef[i, :, CELLS - 128 :], 64, 1))
        strip.append(jnp.where(lane < 64, inner, around[i]))

    def border(m, carry):
        for group in range(4):
            into = pl.ds(pl.multiple_of(m * KL + 8 * group, 8), 8)
            moved = [
                transport(edge[m, f * KL + 8 * group : f * KL + 8 * group + 8, :], *strip)
                for f in range(F)
            ]
            for f, made in enumerate(coupled(moved)):
                first = states[f, into, 0:128]
                states[f, into, 0:128] = jnp.where(lane < 4, made, first)
                last = states[f, into, CELLS - 128 :]
                states[f, into, CELLS - 128 :] = jnp.where(lane >= 124, pltpu.roll(made, 64, 1), last)
        return carry

    for m in range(2):
        border(m, 0)


    def answer(r):
        back_y = lax.rem(y + 4 - r // 2, 4)
        back_row = back_y // 2 * 16 + z * 4 + x
        for i in range(4):
            source = r * 8 + i // 2 * 4 + i % 2 * 2 + core
            itself = jnp.logical_and(source == cells, core == 0)

            @pl.when(jnp.logical_not(itself))
            def _():
                pltpu.make_async_remote_copy(
                    src_ref=n0.at[r], dst_ref=n3.at[back_row], send_sem=back_send.at[0],
                    recv_sem=back_recv.at[0],
                    device_id={"cells": source, "members": lax.rem(back_y, 2)},
                ).start()

            @pl.when(itself)
            def _():
                pltpu.make_async_copy(n0.at[r], n3.at[back_row], back_recv.at[0]).start()

    def plane_at(t):
        step = t + t // 2 - 2 * (t // 3)
        return lax.rem(y + 4 - step, 4)

    def finish(plane, turn):
        anomalies = [[] for _ in range(8)]
        crossed = [cross_s[8 * g : 8 * g + 8, :] for g in range(8)]
        for pair in range(2):
            r = 2 * plane + pair
            found = [raw[turn, 8 * g : 8 * g + 8, 128 * pair : 128 * pair + 128] for g in range(8)]
            total = found[0]
            for g in range(1, 8):
                total = total + found[g]
            center = jnp.sum(total, axis=0, keepdims=True) / K
            observed = keep[turn, pair : pair + 1, :]
            scale = keep[turn, 2 + pair : 3 + pair, :]
            row = (observed - center) * scale
            n0[r] = row
            for g in range(8):
                made = (found[g] - center) * scale
                anomalies[g].append(made)
                crossed[g] = crossed[g] + made * row
        stacked = jnp.concatenate([jnp.concatenate(a, axis=1) for a in anomalies], axis=0)
        gram_s[...] += lax.dot_general(
            stacked, stacked, (((1,), (1,)), ((), ())), precision=HIGHEST, preferred_element_type=F32
        )
        for g in range(8):
            cross_s[8 * g : 8 * g + 8, :] = crossed[g]

    def arrived(plane):
        for pair in range(2):
            r = 2 * plane + pair
            whole(m3.at[pl.ds(4 * r, 4)], ask_recv.at[r]).wait()

    def prepare(plane, turn):
        for pair in range(2):
            rows = m3[pl.ds(4 * (2 * plane + pair), 4)].reshape(4, 128)
            rows = jnp.concatenate([rows, rows], axis=0)
            asked = []
            for q in range(3):
                got = lanes_of(rows, 32 * q + slot)
                got = jnp.where(which == sub, got, 0.0)
                asked.append(jnp.sum(got, axis=0, keepdims=True))
            places[pair : pair + 1, :] = asked[0]
            keep[turn, pair : pair + 1, :] = asked[1]
            keep[turn, 2 + pair : 3 + pair, :] = asked[2]

    def pick(t, carry):
        turn = lax.rem(t, 2)

        @pl.when(t > 1)
        def _():
            before = plane_at(t - 2)
            answer(2 * before)
            answer(2 * before + 1)

        @pl.when(t < 3)
        def _():
            arrived(plane_at(t + 1))

        finish(plane_at(lax.rem(t + 3, 4)), 1 - turn)
        indices = [places[pair : pair + 1, :] for pair in range(2)]
        prepare(plane_at(lax.rem(t + 1, 4)), 1 - turn)
        for pair in range(2):
            index = jnp.broadcast_to(indices[pair], (8, 128)).astype(I32)
            low = index & 127
            high = index // 128
            found = [jnp.zeros((8, 128), F32)] * 8
            for c in range(32):
                here = high == c
                for g in range(8):
                    tile = states[c // 8, 8 * g : 8 * g + 8, (c % 8) * 128 : (c % 8) * 128 + 128]
                    found[g] = jnp.where(here, lanes_of(tile, low), found[g])
            for g in range(8):
                raw[turn, 8 * g : 8 * g + 8, 128 * pair : 128 * pair + 128] = found[g]
        return carry

    arrived(y)
    prepare(y, 0)
    lax.fori_loop(0, 4, pick, 0)
    finish(plane_at(3), 1)

    gram = gram_s[...]
    row32 = lax.broadcasted_iota(I32, (32, 32), 0)
    col32 = lax.broadcasted_iota(I32, (32, 32), 1)
    last_block = gram[32:64, 32:64]
    triangles = jnp.where(col32 >= row32, gram[0:32, 0:32], last_block)
    diagonal = jnp.sum(jnp.where(col32 == row32, last_block, 0.0), axis=0, keepdims=True)
    crosses = jnp.sum(jnp.transpose(cross_s[...]), axis=0, keepdims=True)
    blocks = jnp.concatenate([triangles, gram[0:32, 32:64]], axis=1)
    first_at = lax.rem(y, 2) * 4 + early_at
    g1[first_at] = jnp.concatenate([blocks[0:16], blocks[16:32]], axis=1)
    e1[first_at] = jnp.concatenate([diagonal, crosses, jnp.zeros((1, 32), F32)], axis=1)

    for device in group1:
        for i, ref in enumerate((g1, e1)):
            pltpu.make_async_remote_copy(
                src_ref=ref.at[first_at], dst_ref=ref.at[first_at], send_sem=plane_send.at[i],
                recv_sem=plane_recv.at[i], device_id=device,
            ).start()
    for t in (2, 3):
        answer(2 * plane_at(t))
        answer(2 * plane_at(t) + 1)

    for f in range(F):
        full = states[f]
        head = full.astype(jnp.bfloat16)
        split[f, 0:K, :] = head
        split[f, K : 2 * K, :] = (full - head.astype(F32)).astype(jnp.bfloat16)

    whole(g1.at[pl.ds(0, 7)], plane_recv.at[0]).wait()
    whole(e1.at[pl.ds(0, 7)], plane_recv.at[1]).wait()

    def summed(ref):
        return ((ref[0] + ref[1]) + (ref[2] + ref[3])) + ((ref[4] + ref[5]) + (ref[6] + ref[7]))

    second_at = y // 2 * 4 + late_at
    g2[second_at] = summed(g1)
    e2[second_at] = summed(e1)
    for device in group2:
        for i, ref in enumerate((g2, e2)):
            pltpu.make_async_remote_copy(
                src_ref=ref.at[second_at], dst_ref=ref.at[second_at], send_sem=plane_send.at[2 + i],
                recv_sem=plane_recv.at[2 + i], device_id=device,
            ).start()
    whole(g2.at[pl.ds(0, 7)], plane_recv.at[2]).wait()
    whole(e2.at[pl.ds(0, 7)], plane_recv.at[3]).wait()
    gc[core] = summed(g2)
    ec[core] = summed(e2)
    adding_row = copy_to(ec.at[core], ec.at[core], 4, pair_id)
    adding = copy_to(gc.at[core], gc.at[core], 3, pair_id)

    whole(n3, back_recv.at[0]).wait()
    shift = 64 * lax.rem(z, 2) + 32 * (x // 2)
    totals = [jnp.zeros((8, 128), F32)] * 2
    for g in range(4):
        rows = n3[8 * g : 8 * g + 8].reshape(8, 128)
        begin = starts_s[8 * g : 8 * g + 8, :]
        number = counts_s[8 * g : 8 * g + 8, :]
        for t in range(2):
            rank = lane + 128 * t - begin
            good = (rank >= 0) & (rank < number)
            got = lanes_of(rows, (rank + shift) & 127)
            totals[t] = totals[t] + jnp.where(good, got, 0.0)
    for t in range(2):
        part[core, t] = jnp.sum(totals[t], axis=0, keepdims=True)
    joined = copy_to(part.at[core], part.at[core], 7, pair_id)

    adding.wait_recv()
    adding_row.wait_recv()
    total = gc[0] + gc[1]
    extra = ec[0] + ec[1]

    upright = jnp.concatenate([total, pltpu.roll(total, 64, 1)], axis=0)
    turned = jnp.transpose(upright)
    diagonals = jnp.broadcast_to(extra, (8, 128))
    a = []
    for h in range(8):
        at = 8 * h % 32
        own_rows = upright[at : at + 8]
        flipped = jnp.concatenate([turned[at : at + 8], jnp.zeros((8, 96), F32)], axis=1)
        if h < 4:
            packed = jnp.where(lane >= 32, own_rows, jnp.where(lane >= sub + at, own_rows, flipped))
        else:
            corner = jnp.where(lane < sub + at, own_rows, jnp.where(lane == sub + at, diagonals, flipped))
            left = jnp.concatenate([turned[8 * h : 8 * h + 8], jnp.zeros((8, 96), F32)], axis=1)
            packed = jnp.where(lane < 32, left, pltpu.roll(corner, 32, 1))
        packed = jnp.where(lane == sub + 8 * h, packed + (K - 1.0), packed)
        a.append(jnp.where(lane < K, packed, 0.0))
    inv = []
    for g in range(8):
        first = 8 * g
        block = a[g]
        inside = (lane >= first) & (lane < first + 8)

        def column(rows, j):
            return jnp.broadcast_to(rows[:, first + j : first + j + 1], (8, 128))

        def spread_row(rows, i):
            return jnp.broadcast_to(rows[i : i + 1, :], (8, 128))

        columns = [column(block, j) for j in range(8)]
        d = {(i, j): spread_row(columns[j], i) for j in range(8) for i in range(j, 8)}
        over, low = [], {}
        for k in range(8):
            over.append(1.0 / d[k, k])
            for i in range(k + 1, 8):
                low[i, k] = d[i, k] * over[k]
            for j in range(k + 1, 8):
                for i in range(j, 8):
                    d[i, j] = d[i, j] - low[i, k] * d[j, k]
        m = {}
        for i in range(8):
            for j in range(i):
                total_ij = low[i, j]
                for e in range(j + 1, i):
                    total_ij = total_ij + low[i, e] * m[e, j]
                m[i, j] = -total_ij
        with_unit = jnp.where(inside, jnp.where(lane == sub + first, 1.0, 0.0), block)
        plain = [spread_row(with_unit, i) for i in range(8)]
        rows = []
        for i in range(8):
            made = plain[i]
            for e in range(i):
                made = made + m[i, e] * plain[e]
            rows.append(made)
        scaled = [rows[i] * over[i] for i in range(8)]
        solved = []
        for i in range(8):
            made = scaled[i]
            for e in range(i + 1, 8):
                made = made + m[e, i] * scaled[e]
            solved.append(made)
        for h in range(g + 1, 8):
            fresh = jnp.where(inside, 0.0, a[h])
            for i in range(8):
                fresh = fresh - column(a[h], i) * solved[i]
            a[h] = fresh
        final = jnp.zeros((8, 128), F32)
        for i in range(8):
            final = jnp.where(sub == i, rows[i] * jnp.sqrt(over[i]), final)
        inv.append(jnp.where(lane <= sub + first, final, 0.0))
    cross_row = jnp.where(lane[0:1] < K, pltpu.roll(diagonals, 96, 1)[0:1], 0.0)
    columns = jnp.zeros((8, 128), F32)
    weights = jnp.zeros((8, 128), F32)
    means = []
    for h in range(8):
        columns = columns + inv[h]
        means.append(jnp.sum(inv[h], axis=1, keepdims=True) / K)
        carried = jnp.sum(inv[h] * cross_row, axis=1, keepdims=True)
        weights = weights + inv[h] * carried
    column_mean = jnp.sum(columns, axis=0, keepdims=True) / K
    weight_row = jnp.sum(weights, axis=0, keepdims=True)
    grand = jnp.sum(column_mean, axis=1, keepdims=True) / K
    shifted = weight_row - jnp.sum(weight_row, axis=1, keepdims=True) / K + 1.0 / K
    for h in range(8):
        inner = inv[h] - means[h] - column_mean + grand
        rows = shifted + math.sqrt(K - 1.0) * inner
        mix[8 * h : 8 * h + 8, :] = jnp.where(lane < K, rows, pltpu.roll(rows, 64, 1))

    own = mix[pl.ds(pl.multiple_of(core * KL, KL), KL), :]
    head = own.astype(jnp.bfloat16)
    tail = (own - head.astype(F32)).astype(jnp.bfloat16)
    both = jnp.concatenate([head, tail], axis=0)
    for f in range(F):
        product = jnp.dot(both, split[f], preferred_element_type=F32)
        out[f] = product[0:KL] + product[KL : 2 * KL]

    joined.wait_recv()
    for t in range(2):
        innov_out[:, 128 * t : 128 * t + 128] = part[0, t] + part[1, t]
    for made in sent:
        if made is not swap:
            made.wait_send()
    for ref, sem in (
        (m3.at[pl.ds(0, 31)], ask_send), (n3.at[pl.ds(0, 31)], back_send),
    ):
        whole(ref, sem.at[0]).wait()

    @pl.when(jnp.logical_not(alone))
    def _():
        whole(m3.at[0], ask_send.at[0]).wait()
        whole(n3.at[0], back_send.at[0]).wait()

    for side, _, sends, _ in sides:

        @pl.when(sends)
        def _():
            whole(halo_in.at[side], halo_send.at[side]).wait()

    for i, ref in enumerate((g1, e1, g2, e2)):
        whole(ref.at[pl.ds(0, 7)], plane_send.at[i]).wait()


def write_out(by_field, innovation, out_hbm, innov_hbm, sems):
    made = [pltpu.make_async_copy(innovation, innov_hbm, sems.at[F])]
    made += [pltpu.make_async_copy(by_field.at[f], out_hbm.at[:, f], sems.at[f]) for f in range(F)]
    for copy in made:
        copy.start()
    for copy in made:
        copy.wait()


def shards(
    ensemble, speed, direction, couple, obs_place, obs_field, obs_value, obs_sigma, send_count
):
    vmem = pl.BlockSpec(memory_space=pltpu.VMEM)
    hbm = pl.BlockSpec(memory_space=pl.ANY)
    row = lambda a: a.reshape(1, -1)
    analysis, innovation = pl.pallas_call(
        kernel,
        out_shape=(
            pltpu.VMEM((F, KL, CELLS), F32),
            pltpu.VMEM((1, 256), F32),
        ),
        in_specs=[hbm] * 9,
        out_specs=(vmem, vmem),
        scratch_shapes=[
            pltpu.VMEM((F * KL, CELLS), F32),
            pltpu.VMEM((1, CELLS), F32),
            pltpu.VMEM((1, CELLS), I32),
            pltpu.SMEM((F, F), F32),
            pltpu.VMEM((1, 256), I32),
            pltpu.VMEM((1, 256), I32),
            pltpu.VMEM((1, 256), F32),
            pltpu.VMEM((1, 256), F32),
            pltpu.VMEM((1, 64), I32),
            pltpu.VMEM((F, K, CELLS), F32),
            pltpu.VMEM((F, 2 * K, CELLS), jnp.bfloat16),
            pltpu.VMEM((3, 8, CELLS), F32),
            pltpu.VMEM((2, 16, 128), F32),
            pltpu.VMEM((2, 2, 16, 128), F32),
            pltpu.VMEM((2, 128, 128), F32),
            pltpu.VMEM((2, 128, 128), F32),
            pltpu.VMEM((2, 8, 128), F32),
            pltpu.VMEM((8, 128), F32),
            pltpu.VMEM((2, K, 256), F32),
            pltpu.VMEM((32, 1, 128), F32),
            pltpu.VMEM((32, 1, 128), F32),
            pltpu.VMEM((32, 128), I32),
            pltpu.VMEM((32, 128), I32),
            pltpu.VMEM((K, K), F32),
            pltpu.VMEM((K, 128), F32),
            pltpu.VMEM((8, 1, 128), F32),
            pltpu.VMEM((32, 1, 128), F32),
            pltpu.VMEM((2, 2, 1, 128), F32),
            pltpu.VMEM((8, 16, 128), F32),
            pltpu.VMEM((8, 16, 128), F32),
            pltpu.VMEM((2, 16, 128), F32),
            pltpu.VMEM((8, 1, 128), F32),
            pltpu.VMEM((8, 1, 128), F32),
            pltpu.VMEM((2, 1, 128), F32),
            pltpu.VMEM((K, 128), F32),
            pltpu.SemaphoreType.DMA((8,)),
            pltpu.SemaphoreType.DMA((8,)),
            pltpu.SemaphoreType.DMA((12,)),
            pltpu.SemaphoreType.DMA((1,)),
            pltpu.SemaphoreType.DMA((8,)),
            pltpu.SemaphoreType.DMA((1,)),
            pltpu.SemaphoreType.DMA((1,)),
            pltpu.SemaphoreType.DMA((4,)),
            pltpu.SemaphoreType.DMA((4,)),
            pltpu.SemaphoreType.DMA((2,)),
            pltpu.SemaphoreType.DMA((2,)),
        ],
        compiler_params=pltpu.CompilerParams(collective_id=0, has_side_effects=True),
    )(
        ensemble, row(speed), row(direction), couple, row(obs_place), row(obs_field),
        row(obs_value), row(obs_sigma), send_count,
    )
    analysis, innovation = pl.pallas_call(
        write_out,
        out_shape=(
            jax.ShapeDtypeStruct((KL, F, CELLS), F32),
            jax.ShapeDtypeStruct((1, 256), F32),
        ),
        in_specs=[vmem, vmem],
        out_specs=(hbm, hbm),
        scratch_shapes=[pltpu.SemaphoreType.DMA((F + 1,))],
    )(*(pltpu.with_memory_space_constraint(a, pltpu.VMEM) for a in (analysis, innovation)))
    return analysis, innovation.reshape(256)


def solution(mesh):
    return jax.shard_map(
        shards,
        mesh=mesh,
        in_specs=(
            P("members", None, "cells"),
            P("cells"),
            P("cells"),
            P(),
            P("cells"),
            P("cells"),
            P("cells"),
            P("cells"),
            P("cells", None),
        ),
        out_specs=(P("members", None, "cells"), P("cells")),
        check_vma=False,
    )
```

```python
import math

import jax
import jax.numpy as jnp
from jax import lax
from jax.experimental import pallas as pl
from jax.experimental.pallas import tpu as pltpu
from jax.sharding import PartitionSpec as P

STEPS = 4
DIFFUSION = 0.05
F = 4
K = 64
KL = 32
CELLS = 1024
FAR = (2, 1, 3, 0)
PLANE = [(dx, dz) for dx in FAR for dz in FAR]
F32 = jnp.float32
I32 = jnp.int32
HIGHEST = lax.Precision.HIGHEST


def lanes_of(table, index):
    return jnp.take_along_axis(table, index, axis=1, mode="promise_in_bounds")


def kernel(
    ens_hbm, speed_hbm, direction_hbm, couple_hbm, place_hbm, field_hbm, value_hbm, sigma_hbm,
    counts_hbm, out, innov_out,
    ens, speed, direction, couple, place, field, value, sigma, counts,
    states, split, coef, halo_out, halo_in, edge, base, keep, places, raw,
    m0, m3, starts_s, counts_s, gram_s, cross_s,
    n0, n3, part, g1, g2, gc, e1, e2, ec, mix, send, recv, bulk,
    ask_send, ask_recv, back_send, back_recv, plane_send, plane_recv, halo_send, halo_recv,
):
    cells = lax.axis_index("cells")
    core = lax.axis_index("members")
    x = lax.rem(cells, 4)
    z = lax.rem(cells // 4, 4)
    y = cells // 16
    left_id = lax.rem(cells + 63, 64)
    right_id = lax.rem(cells + 1, 64)
    pair_id = {"cells": cells, "members": 1 - core}
    xs = [lax.rem(x + d, 4) for d in range(4)]
    zs = [lax.rem(z + d, 4) for d in range(4)]
    ys = [lax.rem(y + d, 4) for d in range(4)]
    parity = lax.rem(x, 2)
    in_plane = {(dx, dz): zs[dz] * 4 + xs[dx] for dx, dz in PLANE}
    own_ys = [lax.rem(y + core + 2 * i, 4) for i in range(2)]
    served_x = [lax.rem(x + lax.rem(x + core, 2) + 2 * i, 4) for i in range(2)]
    alone = core + parity == 0
    early_at = x + core * (z - x)
    late_at = z + core * (x - z)
    early_stride = 1 + 3 * core
    late_stride = 4 - 3 * core
    beside = y + 1 - 2 * lax.rem(y, 2)
    group1, group2 = [], []
    for across, step in ((1, 2), (0, 2), (1, 1), (1, 3), (0, 1), (0, 3), (1, 0)):
        along = lax.rem(early_at + step, 4) * early_stride + late_at * late_stride
        group1.append({"cells": (beside if across else y) * 16 + along, "members": core})
        along = lax.rem(late_at + step, 4) * late_stride + early_at * early_stride
        group2.append({"cells": (3 - y if across else y) * 16 + along, "members": core})
    asked_of = [
        (own_ys[i] * 16 + in_plane[dx, dz], i * 16 + in_plane[dx, dz], (dx, dz, i))
        for i in (1, 0) for dx, dz in PLANE
    ]

    barrier = pltpu.get_barrier_semaphore()

    for target, _, at in asked_of[:-1]:
        pl.semaphore_signal(barrier, inc=1, device_id={"cells": target, "members": parity})
    for dy in (2, 1, 3, 0):
        for dz in FAR:
            for i in (1, 0):
                if (dy, dz, i) != (0, 0, 0):
                    target = ys[dy] * 16 + zs[dz] * 4 + served_x[i]
                    pl.semaphore_signal(
                        barrier, inc=1, device_id={"cells": target, "members": dy % 2}
                    )
    for device in group1 + group2:
        pl.semaphore_signal(barrier, inc=1, device_id=device)
    @pl.when(jnp.logical_not(alone))
    def _():
        pl.semaphore_signal(
            barrier, inc=1, device_id={"cells": asked_of[-1][0], "members": parity}
        )

    @pl.when(jnp.logical_not(alone))
    def _():
        pl.semaphore_signal(
            barrier, inc=1, device_id={"cells": y * 16 + z * 4 + served_x[0], "members": 0}
        )

    pl.semaphore_signal(barrier, inc=1, device_id=pair_id)
    for neighbour in (left_id, right_id):
        for to in range(2):
            pl.semaphore_signal(barrier, inc=1, device_id={"cells": neighbour, "members": to})
    small = (
        (counts_hbm, counts), (place_hbm, place), (field_hbm, field), (value_hbm, value),
        (sigma_hbm, sigma), (speed_hbm, speed), (direction_hbm, direction), (couple_hbm, couple),
    )
    early = [pltpu.make_async_copy(src, dst, bulk.at[F + i]) for i, (src, dst) in enumerate(small)]
    loads = [
        pltpu.make_async_copy(ens_hbm.at[:, f], ens.at[pl.ds(f * KL, KL)], bulk.at[f]) for f in range(F)
    ]
    for made in early:
        made.start()
    for made in loads:
        made.start()

    sent = []

    def copy_to(src, dst, at, device):
        made = pltpu.make_async_remote_copy(
            src_ref=src, dst_ref=dst, send_sem=send.at[at], recv_sem=recv.at[at], device_id=device
        )
        made.start()
        sent.append(made)
        return made

    def whole(ref, sem):
        return pltpu.make_async_copy(ref, ref, sem)

    lane = lax.broadcasted_iota(I32, (8, 128), 1)
    sub = lax.broadcasted_iota(I32, (8, 128), 0)
    lane64 = lax.broadcasted_iota(I32, (8, 64), 1)
    sub64 = lax.broadcasted_iota(I32, (8, 64), 0)

    for made in early:
        made.wait()
    flat = (field[...] * CELLS + place[...]).astype(F32)
    inverse = 1.0 / sigma[...]
    tables = []
    for quantity in (flat, value[...], inverse):
        tables.append([
            jnp.broadcast_to(quantity[:, h * 128 : (h + 1) * 128], (8, 128)) for h in (0, 1)
        ])
    count_row = jnp.broadcast_to(counts[...], (8, 64))

    def start_and_count(owner):
        begin = jnp.sum(jnp.where(lane64 < owner, count_row, 0), axis=1, keepdims=True)
        number = jnp.sum(jnp.where(lane64 == owner, count_row, 0), axis=1, keepdims=True)
        return begin, number

    slot = lane % 32
    which = lane // 32
    for g in range(4):
        row = sub64 + 8 * g
        owner_y = own_ys[g // 2]
        begin, number = start_and_count(owner_y * 16 + row % 16)
        begin = jnp.broadcast_to(begin, (8, 128))
        number = jnp.broadcast_to(number, (8, 128))
        starts_s[8 * g : 8 * g + 8, :] = begin
        counts_s[8 * g : 8 * g + 8, :] = number
        position = begin + slot
        low = position & 127
        second = position >= 128
        found = jnp.zeros((8, 128), F32)
        for q in range(3):
            got = jnp.where(second, lanes_of(tables[q][1], low), lanes_of(tables[q][0], low))
            found = jnp.where(which == q, got, found)
        found = jnp.where(slot < number, found, 0.0)
        m0[8 * g : 8 * g + 8] = found.reshape(8, 1, 128)

    for made in loads:
        made.wait()
    toward_left = speed[...] * direction[...].astype(F32)
    for side, first in ((0, 896), (1, 0)):
        turned = jnp.transpose(ens[:, first : first + 128])
        halo_out[side, 0:8, :] = turned[120:128, :] if side == 0 else turned[0:8, :]
        halo_out[side, 8:9, :] = speed[:, first : first + 128]
        halo_out[side, 9:10, :] = toward_left[:, first : first + 128]
        halo_out[side, 10:16, :] = jnp.zeros((6, 128), F32)
    wide = lax.broadcasted_iota(I32, (F * KL, 128), 1)
    base[core] = jnp.where(wide < 32, ens[:, 0:128], pltpu.roll(ens[:, CELLS - 128 :], 64, 1))

    for m in range(2):
        edge[m] = jnp.zeros((128, 128), F32)
    gram_s[...] = jnp.zeros((K, K), F32)
    cross_s[...] = jnp.zeros((K, 128), F32)
    keep[...] = jnp.zeros((2, 8, 128), F32)
    raw[...] = jnp.zeros((2, K, 256), F32)
    gain = [[couple[f, g] + (1.0 if f == g else 0.0) for g in range(F)] for f in range(F)]
    for _ in range(2):
        gain = [
            [sum(gain[f][e] * gain[e][g] for e in range(F)) for g in range(F)] for f in range(F)
        ]
    speed_row = speed[...]
    coef[0, :, 0:CELLS] = jnp.broadcast_to(1.0 - 2.0 * DIFFUSION - speed_row, (8, CELLS))
    coef[1, :, 0:CELLS] = jnp.broadcast_to(toward_left + DIFFUSION, (8, CELLS))
    coef[2, :, 0:CELLS] = jnp.broadcast_to(speed_row - toward_left + DIFFUSION, (8, CELLS))

    def transport(u, centre, from_left, from_right):
        width = u.shape[1]
        for _ in range(STEPS):
            u = (
                centre * u
                + from_left * pltpu.roll(u, 1, 1)
                + from_right * pltpu.roll(u, width - 1, 1)
            )
        return u

    def coupled(moved):
        return [sum(gain[f][g] * moved[g] for g in range(F)) for f in range(F)]

    def interior(group, carry):
        rows = pl.multiple_of(group * 8, 8)
        into = pl.ds(pl.multiple_of(core * KL + rows, 8), 8)
        moved = [
            transport(
                ens[pl.ds(f * KL + rows, 8), :],
                coef[0, :, 0:CELLS], coef[1, :, 0:CELLS], coef[2, :, 0:CELLS],
            )
            for f in range(F)
        ]
        for f, made in enumerate(coupled(moved)):
            states[f, into, :] = made
        return carry

    lax.fori_loop(0, 1, interior, 0)

    pl.semaphore_wait(barrier, 83 - 2 * jnp.where(alone, 1, 0))

    sides = ((0, right_id, cells < 63, cells > 0), (1, left_id, cells > 0, cells < 63))
    for side, neighbour, sends, _ in sides:

        @pl.when(sends)
        def _():
            for to in range(2):
                pltpu.make_async_remote_copy(
                    src_ref=halo_out.at[side], dst_ref=halo_in.at[side, core],
                    send_sem=halo_send.at[side], recv_sem=halo_recv.at[side],
                    device_id={"cells": neighbour, "members": to},
                ).start()

        @pl.when(jnp.logical_not(sends))
        def _():
            halo_in[1 - side] = jnp.zeros((2, 16, 128), F32)

    based = copy_to(base.at[core], base.at[core], 0, pair_id)
    source_at = y * 8 + z * 2 + x // 2

    def ask(target, row):
        pltpu.make_async_remote_copy(
            src_ref=m0.at[row], dst_ref=m3.at[source_at], send_sem=ask_send.at[0],
            recv_sem=ask_recv.at[cells // 8], device_id={"cells": target, "members": parity},
        ).start()

    for target, row, at in asked_of[:-1]:
        ask(target, row)

    @pl.when(jnp.logical_not(alone))
    def _():
        ask(*asked_of[-1][:2])

    @pl.when(alone)
    def _():
        pltpu.make_async_copy(m0.at[asked_of[-1][1]], m3.at[source_at], ask_recv.at[cells // 8]).start()

    lax.fori_loop(1, 4, interior, 0)

    mine = states.at[:, pl.ds(pl.multiple_of(core * KL, KL), KL), :]
    swap = copy_to(mine, mine, 2, pair_id)

    based.wait_recv()
    for side, _, _, receives in sides:

        @pl.when(receives)
        def _():
            whole(halo_in.at[side], halo_recv.at[side]).wait()

    swap.wait()
    has_left = jnp.where(cells > 0, 1.0, 0.0).astype(F32)
    has_right = jnp.where(cells < 63, 1.0, 0.0).astype(F32)
    for m in range(2):
        edge[m, 64:72, :] = halo_in[1, m, 0:8, :] * has_right
        edge[m, 120:128, :] = halo_in[0, m, 0:8, :] * has_left
        edge[m] = jnp.where(wide < 64, base[m], jnp.transpose(edge[m]))
    beyond = lane < 96
    present = jnp.where(beyond, has_right, has_left)

    def outside(row):
        after = jnp.broadcast_to(halo_in[1, 0, row : row + 1, :], (8, 128))
        before = jnp.broadcast_to(halo_in[0, 0, row : row + 1, :], (8, 128))
        return jnp.where(beyond, pltpu.roll(after, 64, 1), before)

    edge_speed, edge_left = outside(8), outside(9)
    around = (
        present * (1.0 - 2.0 * DIFFUSION - edge_speed),
        present * (edge_left + DIFFUSION),
        present * (edge_speed - edge_left + DIFFUSION),
    )
    strip = []
    for i in range(3):
        inner = jnp.where(lane < 32, coef[i, :, 0:128], pltpu.roll(coef[i, :, CELLS - 128 :], 64, 1))
        strip.append(jnp.where(lane < 64, inner, around[i]))

    def border(m, carry):
        for group in range(4):
            into = pl.ds(pl.multiple_of(m * KL + 8 * group, 8), 8)
            moved = [
                transport(edge[m, f * KL + 8 * group : f * KL + 8 * group + 8, :], *strip)
                for f in range(F)
            ]
            for f, made in enumerate(coupled(moved)):
                first = states[f, into, 0:128]
                states[f, into, 0:128] = jnp.where(lane < 4, made, first)
                last = states[f, into, CELLS - 128 :]
                states[f, into, CELLS - 128 :] = jnp.where(lane >= 124, pltpu.roll(made, 64, 1), last)
        return carry

    for m in range(2):
        border(m, 0)


    def answer(r):
        back_y = lax.rem(y + 4 - r // 2, 4)
        back_row = back_y // 2 * 16 + z * 4 + x
        for i in range(4):
            source = r * 8 + i // 2 * 4 + i % 2 * 2 + core
            itself = jnp.logical_and(source == cells, core == 0)

            @pl.when(jnp.logical_not(itself))
            def _():
                pltpu.make_async_remote_copy(
                    src_ref=n0.at[r], dst_ref=n3.at[back_row], send_sem=back_send.at[0],
                    recv_sem=back_recv.at[0],
                    device_id={"cells": source, "members": lax.rem(back_y, 2)},
                ).start()

            @pl.when(itself)
            def _():
                pltpu.make_async_copy(n0.at[r], n3.at[back_row], back_recv.at[0]).start()

    def plane_at(t):
        step = t + t // 2 - 2 * (t // 3)
        return lax.rem(y + 4 - step, 4)

    def finish(plane, turn):
        anomalies = [[] for _ in range(8)]
        crossed = [cross_s[8 * g : 8 * g + 8, :] for g in range(8)]
        for pair in range(2):
            r = 2 * plane + pair
            found = [raw[turn, 8 * g : 8 * g + 8, 128 * pair : 128 * pair + 128] for g in range(8)]
            total = found[0]
            for g in range(1, 8):
                total = total + found[g]
            center = jnp.sum(total, axis=0, keepdims=True) / K
            observed = keep[turn, pair : pair + 1, :]
            scale = keep[turn, 2 + pair : 3 + pair, :]
            row = (observed - center) * scale
            n0[r] = row
            for g in range(8):
                made = (found[g] - center) * scale
                anomalies[g].append(made)
                crossed[g] = crossed[g] + made * row
        stacked = jnp.concatenate([jnp.concatenate(a, axis=1) for a in anomalies], axis=0)
        gram_s[...] += lax.dot_general(
            stacked, stacked, (((1,), (1,)), ((), ())), precision=HIGHEST, preferred_element_type=F32
        )
        for g in range(8):
            cross_s[8 * g : 8 * g + 8, :] = crossed[g]

    def arrived(plane):
        for pair in range(2):
            r = 2 * plane + pair
            whole(m3.at[pl.ds(4 * r, 4)], ask_recv.at[r]).wait()

    def prepare(plane, turn):
        for pair in range(2):
            rows = m3[pl.ds(4 * (2 * plane + pair), 4)].reshape(4, 128)
            rows = jnp.concatenate([rows, rows], axis=0)
            asked = []
            for q in range(3):
                got = lanes_of(rows, 32 * q + slot)
                got = jnp.where(which == sub, got, 0.0)
                asked.append(jnp.sum(got, axis=0, keepdims=True))
            places[pair : pair + 1, :] = asked[0]
            keep[turn, pair : pair + 1, :] = asked[1]
            keep[turn, 2 + pair : 3 + pair, :] = asked[2]

    def pick(t, carry):
        turn = lax.rem(t, 2)

        @pl.when(t > 1)
        def _():
            before = plane_at(t - 2)
            answer(2 * before)
            answer(2 * before + 1)

        @pl.when(t < 3)
        def _():
            arrived(plane_at(t + 1))

        finish(plane_at(lax.rem(t + 3, 4)), 1 - turn)
        indices = [places[pair : pair + 1, :] for pair in range(2)]
        prepare(plane_at(lax.rem(t + 1, 4)), 1 - turn)
        for pair in range(2):
            index = jnp.broadcast_to(indices[pair], (8, 128)).astype(I32)
            low = index & 127
            high = index // 128
            found = [jnp.zeros((8, 128), F32)] * 8
            for c in range(32):
                here = high == c
                for g in range(8):
                    tile = states[c // 8, 8 * g : 8 * g + 8, (c % 8) * 128 : (c % 8) * 128 + 128]
                    found[g] = jnp.where(here, lanes_of(tile, low), found[g])
            for g in range(8):
                raw[turn, 8 * g : 8 * g + 8, 128 * pair : 128 * pair + 128] = found[g]
        return carry

    arrived(y)
    prepare(y, 0)
    lax.fori_loop(0, 4, pick, 0)
    finish(plane_at(3), 1)

    gram = gram_s[...]
    row32 = lax.broadcasted_iota(I32, (32, 32), 0)
    col32 = lax.broadcasted_iota(I32, (32, 32), 1)
    last_block = gram[32:64, 32:64]
    triangles = jnp.where(col32 >= row32, gram[0:32, 0:32], last_block)
    diagonal = jnp.sum(jnp.where(col32 == row32, last_block, 0.0), axis=0, keepdims=True)
    crosses = jnp.sum(jnp.transpose(cross_s[...]), axis=0, keepdims=True)
    blocks = jnp.concatenate([triangles, gram[0:32, 32:64]], axis=1)
    first_at = lax.rem(y, 2) * 4 + early_at
    g1[first_at] = jnp.concatenate([blocks[0:16], blocks[16:32]], axis=1)
    e1[first_at] = jnp.concatenate([diagonal, crosses, jnp.zeros((1, 32), F32)], axis=1)

    for device in group1:
        for i, ref in enumerate((g1, e1)):
            pltpu.make_async_remote_copy(
                src_ref=ref.at[first_at], dst_ref=ref.at[first_at], send_sem=plane_send.at[i],
                recv_sem=plane_recv.at[i], device_id=device,
            ).start()
    for t in (2, 3):
        answer(2 * plane_at(t))
        answer(2 * plane_at(t) + 1)

    for f in range(F):
        full = states[f]
        head = full.astype(jnp.bfloat16)
        split[f, 0:K, :] = head
        split[f, K : 2 * K, :] = (full - head.astype(F32)).astype(jnp.bfloat16)

    whole(g1.at[pl.ds(0, 7)], plane_recv.at[0]).wait()
    whole(e1.at[pl.ds(0, 7)], plane_recv.at[1]).wait()

    def summed(ref):
        return ((ref[0] + ref[1]) + (ref[2] + ref[3])) + ((ref[4] + ref[5]) + (ref[6] + ref[7]))

    second_at = y // 2 * 4 + late_at
    g2[second_at] = summed(g1)
    e2[second_at] = summed(e1)
    for device in group2:
        for i, ref in enumerate((g2, e2)):
            pltpu.make_async_remote_copy(
                src_ref=ref.at[second_at], dst_ref=ref.at[second_at], send_sem=plane_send.at[2 + i],
                recv_sem=plane_recv.at[2 + i], device_id=device,
            ).start()
    whole(g2.at[pl.ds(0, 7)], plane_recv.at[2]).wait()
    whole(e2.at[pl.ds(0, 7)], plane_recv.at[3]).wait()
    gc[core] = summed(g2)
    ec[core] = summed(e2)
    adding_row = copy_to(ec.at[core], ec.at[core], 4, pair_id)
    adding = copy_to(gc.at[core], gc.at[core], 3, pair_id)

    whole(n3, back_recv.at[0]).wait()
    shift = 64 * lax.rem(z, 2) + 32 * (x // 2)
    totals = [jnp.zeros((8, 128), F32)] * 2
    for g in range(4):
        rows = n3[8 * g : 8 * g + 8].reshape(8, 128)
        begin = starts_s[8 * g : 8 * g + 8, :]
        number = counts_s[8 * g : 8 * g + 8, :]
        for t in range(2):
            rank = lane + 128 * t - begin
            good = (rank >= 0) & (rank < number)
            got = lanes_of(rows, (rank + shift) & 127)
            totals[t] = totals[t] + jnp.where(good, got, 0.0)
    for t in range(2):
        part[core, t] = jnp.sum(totals[t], axis=0, keepdims=True)
    joined = copy_to(part.at[core], part.at[core], 7, pair_id)

    adding.wait_recv()
    adding_row.wait_recv()
    total = gc[0] + gc[1]
    extra = ec[0] + ec[1]

    upright = jnp.concatenate([total, pltpu.roll(total, 64, 1)], axis=0)
    turned = jnp.transpose(upright)
    diagonals = jnp.broadcast_to(extra, (8, 128))
    a = []
    for h in range(8):
        at = 8 * h % 32
        own_rows = upright[at : at + 8]
        flipped = jnp.concatenate([turned[at : at + 8], jnp.zeros((8, 96), F32)], axis=1)
        if h < 4:
            packed = jnp.where(lane >= 32, own_rows, jnp.where(lane >= sub + at, own_rows, flipped))
        else:
            corner = jnp.where(lane < sub + at, own_rows, jnp.where(lane == sub + at, diagonals, flipped))
            left = jnp.concatenate([turned[8 * h : 8 * h + 8], jnp.zeros((8, 96), F32)], axis=1)
            packed = jnp.where(lane < 32, left, pltpu.roll(corner, 32, 1))
        packed = jnp.where(lane == sub + 8 * h, packed + (K - 1.0), packed)
        a.append(jnp.where(lane < K, packed, 0.0))
    inv = []
    for g in range(8):
        first = 8 * g
        block = a[g]
        inside = (lane >= first) & (lane < first + 8)

        def column(rows, j):
            return jnp.broadcast_to(rows[:, first + j : first + j + 1], (8, 128))

        def spread_row(rows, i):
            return jnp.broadcast_to(rows[i : i + 1, :], (8, 128))

        columns = [column(block, j) for j in range(8)]
        d = {(i, j): spread_row(columns[j], i) for j in range(8) for i in range(j, 8)}
        over, low = [], {}
        for k in range(8):
            over.append(1.0 / d[k, k])
            for i in range(k + 1, 8):
                low[i, k] = d[i, k] * over[k]
            for j in range(k + 1, 8):
                for i in range(j, 8):
                    d[i, j] = d[i, j] - low[i, k] * d[j, k]
        m = {}
        for i in range(8):
            for j in range(i):
                total_ij = low[i, j]
                for e in range(j + 1, i):
                    total_ij = total_ij + low[i, e] * m[e, j]
                m[i, j] = -total_ij
        with_unit = jnp.where(inside, jnp.where(lane == sub + first, 1.0, 0.0), block)
        plain = [spread_row(with_unit, i) for i in range(8)]
        rows = []
        for i in range(8):
            made = plain[i]
            for e in range(i):
                made = made + m[i, e] * plain[e]
            rows.append(made)
        scaled = [rows[i] * over[i] for i in range(8)]
        solved = []
        for i in range(8):
            made = scaled[i]
            for e in range(i + 1, 8):
                made = made + m[e, i] * scaled[e]
            solved.append(made)
        for h in range(g + 1, 8):
            fresh = jnp.where(inside, 0.0, a[h])
            for i in range(8):
                fresh = fresh - column(a[h], i) * solved[i]
            a[h] = fresh
        final = jnp.zeros((8, 128), F32)
        for i in range(8):
            final = jnp.where(sub == i, rows[i] * jnp.sqrt(over[i]), final)
        inv.append(jnp.where(lane <= sub + first, final, 0.0))
    cross_row = jnp.where(lane[0:1] < K, pltpu.roll(diagonals, 96, 1)[0:1], 0.0)
    columns = jnp.zeros((8, 128), F32)
    weights = jnp.zeros((8, 128), F32)
    means = []
    for h in range(8):
        columns = columns + inv[h]
        means.append(jnp.sum(inv[h], axis=1, keepdims=True) / K)
        carried = jnp.sum(inv[h] * cross_row, axis=1, keepdims=True)
        weights = weights + inv[h] * carried
    column_mean = jnp.sum(columns, axis=0, keepdims=True) / K
    weight_row = jnp.sum(weights, axis=0, keepdims=True)
    grand = jnp.sum(column_mean, axis=1, keepdims=True) / K
    shifted = weight_row - jnp.sum(weight_row, axis=1, keepdims=True) / K + 1.0 / K
    for h in range(8):
        inner = inv[h] - means[h] - column_mean + grand
        rows = shifted + math.sqrt(K - 1.0) * inner
        mix[8 * h : 8 * h + 8, :] = jnp.where(lane < K, rows, pltpu.roll(rows, 64, 1))

    own = mix[pl.ds(pl.multiple_of(core * KL, KL), KL), :]
    head = own.astype(jnp.bfloat16)
    tail = (own - head.astype(F32)).astype(jnp.bfloat16)
    both = jnp.concatenate([head, tail], axis=0)
    for f in range(F):
        product = jnp.dot(both, split[f], preferred_element_type=F32)
        out[f] = product[0:KL] + product[KL : 2 * KL]

    joined.wait_recv()
    for t in range(2):
        innov_out[:, 128 * t : 128 * t + 128] = part[0, t] + part[1, t]
    for made in sent:
        if made is not swap:
            made.wait_send()
    for ref, sem in (
        (m3.at[pl.ds(0, 31)], ask_send), (n3.at[pl.ds(0, 31)], back_send),
    ):
        whole(ref, sem.at[0]).wait()

    @pl.when(jnp.logical_not(alone))
    def _():
        whole(m3.at[0], ask_send.at[0]).wait()
        whole(n3.at[0], back_send.at[0]).wait()

    for side, _, sends, _ in sides:

        @pl.when(sends)
        def _():
            whole(halo_in.at[side], halo_send.at[side]).wait()

    for i, ref in enumerate((g1, e1, g2, e2)):
        whole(ref.at[pl.ds(0, 7)], plane_send.at[i]).wait()


def write_out(by_field, innovation, out_hbm, innov_hbm, sems):
    made = [pltpu.make_async_copy(innovation, innov_hbm, sems.at[F])]
    made += [pltpu.make_async_copy(by_field.at[f], out_hbm.at[:, f], sems.at[f]) for f in range(F)]
    for copy in made:
        copy.start()
    for copy in made:
        copy.wait()


def shards(
    ensemble, speed, direction, couple, obs_place, obs_field, obs_value, obs_sigma, send_count
):
    vmem = pl.BlockSpec(memory_space=pltpu.VMEM)
    hbm = pl.BlockSpec(memory_space=pl.ANY)
    row = lambda a: a.reshape(1, -1)
    analysis, innovation = pl.pallas_call(
        kernel,
        out_shape=(
            pltpu.VMEM((F, KL, CELLS), F32),
            pltpu.VMEM((1, 256), F32),
        ),
        in_specs=[hbm] * 9,
        out_specs=(vmem, vmem),
        scratch_shapes=[
            pltpu.VMEM((F * KL, CELLS), F32),
            pltpu.VMEM((1, CELLS), F32),
            pltpu.VMEM((1, CELLS), I32),
            pltpu.SMEM((F, F), F32),
            pltpu.VMEM((1, 256), I32),
            pltpu.VMEM((1, 256), I32),
            pltpu.VMEM((1, 256), F32),
            pltpu.VMEM((1, 256), F32),
            pltpu.VMEM((1, 64), I32),
            pltpu.VMEM((F, K, CELLS), F32),
            pltpu.VMEM((F, 2 * K, CELLS), jnp.bfloat16),
            pltpu.VMEM((3, 8, CELLS), F32),
            pltpu.VMEM((2, 16, 128), F32),
            pltpu.VMEM((2, 2, 16, 128), F32),
            pltpu.VMEM((2, 128, 128), F32),
            pltpu.VMEM((2, 128, 128), F32),
            pltpu.VMEM((2, 8, 128), F32),
            pltpu.VMEM((8, 128), F32),
            pltpu.VMEM((2, K, 256), F32),
            pltpu.VMEM((32, 1, 128), F32),
            pltpu.VMEM((32, 1, 128), F32),
            pltpu.VMEM((32, 128), I32),
            pltpu.VMEM((32, 128), I32),
            pltpu.VMEM((K, K), F32),
            pltpu.VMEM((K, 128), F32),
            pltpu.VMEM((8, 1, 128), F32),
            pltpu.VMEM((32, 1, 128), F32),
            pltpu.VMEM((2, 2, 1, 128), F32),
            pltpu.VMEM((8, 16, 128), F32),
            pltpu.VMEM((8, 16, 128), F32),
            pltpu.VMEM((2, 16, 128), F32),
            pltpu.VMEM((8, 1, 128), F32),
            pltpu.VMEM((8, 1, 128), F32),
            pltpu.VMEM((2, 1, 128), F32),
            pltpu.VMEM((K, 128), F32),
            pltpu.SemaphoreType.DMA((8,)),
            pltpu.SemaphoreType.DMA((8,)),
            pltpu.SemaphoreType.DMA((12,)),
            pltpu.SemaphoreType.DMA((1,)),
            pltpu.SemaphoreType.DMA((8,)),
            pltpu.SemaphoreType.DMA((1,)),
            pltpu.SemaphoreType.DMA((1,)),
            pltpu.SemaphoreType.DMA((4,)),
            pltpu.SemaphoreType.DMA((4,)),
            pltpu.SemaphoreType.DMA((2,)),
            pltpu.SemaphoreType.DMA((2,)),
        ],
        compiler_params=pltpu.CompilerParams(collective_id=0, has_side_effects=True),
    )(
        ensemble, row(speed), row(direction), couple, row(obs_place), row(obs_field),
        row(obs_value), row(obs_sigma), send_count,
    )
    analysis, innovation = pl.pallas_call(
        write_out,
        out_shape=(
            jax.ShapeDtypeStruct((KL, F, CELLS), F32),
            jax.ShapeDtypeStruct((1, 256), F32),
        ),
        in_specs=[vmem, vmem],
        out_specs=(hbm, hbm),
        scratch_shapes=[pltpu.SemaphoreType.DMA((F + 1,))],
    )(*(pltpu.with_memory_space_constraint(a, pltpu.VMEM) for a in (analysis, innovation)))
    return analysis, innovation.reshape(256)


def solution(mesh):
    return jax.shard_map(
        shards,
        mesh=mesh,
        in_specs=(
            P("members", None, "cells"),
            P("cells"),
            P("cells"),
            P(),
            P("cells"),
            P("cells"),
            P("cells"),
            P("cells"),
            P("cells", None),
        ),
        out_specs=(P("members", None, "cells"), P("cells")),
        check_vma=False,
    )
```
